256 devices in a mesh: tx: 4 (over z_lo, core), img: 64 (over y, z_hi, x).
Axes of the slice: x: 4, y: 4, z: 8 (z_hi: 4, z_lo: 2; z = z_hi * 2 + z_lo), core: 2. Of those that a mesh axis runs over, the one named last changes fastest.
Arguments:
- encoded: bfloat16 [1024, 1024, 512], P('tx', 'img'), may hold values from -6 to 6
- signs: int32 [1024, 64], replicated, may hold values from -1 to 1, as said below
- tx_block: int32 [64, 16384], P('tx'), may hold values from 0 to 1
- rx_block: int32 [1024, 16384], P(None, 'img'), may hold values from 0 to 2
- apodization: int32 [1024, 16384], P(None, 'img'), may hold values 0 or 1
Outputs:
- image: float32 [16384, 128], P('img', 'tx')
The draws below stay inside these ranges and needn't reach their ends.
Inputs may be any that keep to these rules, and one draw needn't show every extreme that they name: `signs`: every entry is 1 or -1. The columns are 64 distinct columns of the Sylvester Hadamard matrix of order 1024, every row multiplied by its own sign, so that two different columns are orthogonal.
All inputs are finite; a program needn't handle non-finite values. No bound on the sum of `apodization` on one device may be relied on, other than what follows from the above.
Results may differ from the reference program's by a relative error of at most 0.0029.
Values may be sent and summed in bfloat16 or wider, within the bound.
A program may use at most 192 MiB of HBM per device.

```python
import math
import jax
import jax.numpy as jnp
from jax import lax

E = 1024
K = 64
R = 1024
NB = 4
L = 128
LINE_DEV = 256
LINES = 16384
N_IMG = 64


def draw_signs(key, part):
    key_cols = jax.random.fold_in(key, 11)
    key_rows = jax.random.fold_in(key, 23)
    columns = jax.random.permutation(key_cols, E)[:K].astype(jnp.int32)
    row_flips = jax.random.randint(key_rows, (E,), 0, 2).astype(jnp.int32) * 2 - 1
    events = jnp.arange(E, dtype=jnp.int32)
    shared = jnp.bitwise_and(events[:, None], columns[None, :])
    parity = jnp.zeros((E, K), jnp.int32)
    for position in range(int(math.log2(E))):
        parity = parity + jnp.bitwise_and(jnp.right_shift(shared, position), 1)
    sign_value = 1 - 2 * jnp.bitwise_and(parity, 1)
    return (sign_value * row_flips[:, None]).astype(jnp.int32)


def touch_ends(result, own_key, least, top_value):
    longest = result.shape.index(max(result.shape))
    spots = []
    for shift in (0, 1):
        where = [jax.random.randint(jax.random.fold_in(own_key, axis), (), 0, length) for axis, length in enumerate(result.shape)]
        where[longest] = (where[longest] + shift) % result.shape[longest]
        spots.append(tuple(where))
    return result.at[spots[0]].set(least).at[spots[1]].set(top_value)


def shard_levels(key, extent, pieces, low, high):
    loudness = 1.0
    for dim, parts in pieces:
        heights = jax.random.uniform(jax.random.fold_in(jax.random.fold_in(key, 6), dim), (parts,), jnp.float32, low / len(pieces), high / len(pieces))
        loudness = loudness * jnp.repeat(jnp.exp(heights), extent[dim] // parts).reshape((-1,) + (1,) * (len(extent) - 1 - dim))
    return loudness


def normal_values(own_key, extent, deviation, limit, shards=(), held_as=jnp.bfloat16):
    array = deviation * jax.random.normal(own_key, extent, jnp.float32)
    if shards:
        array = array * shard_levels(own_key, extent, shards, -0.22, 0.18)
    return jnp.clip(array, -limit, limit).astype(held_as)


def setup_inputs(seed: int = 0) -> dict:
    key_list = jax.random.split(jax.random.key(seed), 6)
    return {
        "encoded": normal_values(key_list[0], (E, R, NB * L), 1.0, 6.0, ((0, 4), (1, 64))),
        "signs": draw_signs(jax.random.fold_in(key_list[5], 71), 0),
        "tx_block": touch_ends(jax.random.randint(key_list[2], (K, LINES), 0, NB // 2), jax.random.fold_in(key_list[2], 1), 0, (NB // 2) - 1).astype(jnp.int32),
        "rx_block": touch_ends(jax.random.randint(key_list[3], (R, LINES), 0, NB - NB // 2 + 1), jax.random.fold_in(key_list[3], 1), 0, (NB - NB // 2 + 1) - 1).astype(jnp.int32),
        "apodization": touch_ends((jax.random.randint(key_list[4], (R, LINES), 0, 4) < 3).astype(jnp.int32), jax.random.fold_in(key_list[4], 1), 0, 1),
    }


def reference(encoded, signs, tx_block, rx_block, apodization):
    flat = encoded.reshape(E, R * NB * L)
    summed = jnp.dot(signs.T.astype(jnp.bfloat16), flat, preferred_element_type=jnp.float32)
    decoded = (summed * (1.0 / E)).astype(jnp.bfloat16)
    trace_rows = decoded.astype(jnp.float32).reshape(K * R * NB, L)
    levels = jnp.arange(NB, dtype=jnp.int32)

    def one_group(start):
        tx_rows = lax.dynamic_slice_in_dim(tx_block, start, LINE_DEV, 1)
        rx_rows = lax.dynamic_slice_in_dim(rx_block, start, LINE_DEV, 1)
        mask_rows = lax.dynamic_slice_in_dim(apodization, start, LINE_DEV, 1)
        total_block = tx_rows.T[:, :, None] + rx_rows.T[:, None, :]
        chosen = total_block[..., None] == levels
        weight = jnp.where(chosen, mask_rows.T[:, None, :, None].astype(jnp.float32), 0.0)
        weight = weight.reshape(LINE_DEV, K * R * NB)
        return jnp.dot(weight, trace_rows, precision=lax.Precision.HIGHEST, preferred_element_type=jnp.float32)
    starts = jnp.arange(N_IMG, dtype=jnp.int32) * LINE_DEV
    lines = lax.map(one_group, starts).reshape(LINES, L)
    return lines * math.sqrt(E / (K * R))
```

```python
import jax
import jax.numpy as jnp
from jax import lax
from jax.experimental import pallas as pl
from jax.experimental.pallas import tpu as pltpu
from jax.sharding import PartitionSpec as P

MESH = pl.DeviceIdType.MESH
F32 = jnp.float32
BF16 = jnp.bfloat16
LG = 256


def kernel(
    enc_hbm, signs_hbm, tx_hbm, rx_hbm, apo_hbm, out_ref,
    encb, encf, sg, part, rb, zs, zb, da, dt, sh, rxi, rxs, rxa, txi,
    delta, keep, send, ib, ys, yb, zss, zrb,
    ld_enc, ld_rx, ld_sg, ld_tx,
    rx_s, rx_r, fw_s, fw_r, sw_s, sw_r, ze_s, ze_r, xg_s, xg_r,
    ci_s, ci_r, y_s, y_r, z_s, z_r,
):
    tx = lax.axis_index("tx")
    img = lax.axis_index("img")
    zl = tx // 2
    co = tx % 2
    y = img // 16
    zh = (img // 4) % 4
    x = img % 4
    z = zh * 2 + zl
    g = y * 4 + zh

    def dev(xx, yy, zz, cc):
        return {"tx": (zz % 2) * 2 + cc, "img": (yy * 4 + zz // 2) * 4 + xx}

    partner = dev(x, y, z, 1 - co)
    mate = dev(x, y, zh * 2 + (1 - zl), co)
    xr = (x + 1) % 4
    xl = (x + 3) % 4
    right = dev(xr, y, z, co)
    left = dev(xl, y, z, co)

    def rcopy(src, dst, ss, rs, to):
        return pltpu.make_async_remote_copy(
            src_ref=src, dst_ref=dst, send_sem=ss, recv_sem=rs,
            device_id=to, device_id_type=MESH,
        )

    def enc_load(i):
        return pltpu.make_async_copy(
            enc_hbm.at[pl.ds(64 * i, 64)], encb.at[pl.ds(64 * i, 64)], ld_enc.at[i]
        )

    l_rx = pltpu.make_async_copy(rx_hbm, rxi.at[0], ld_rx.at[0])
    l_ap = pltpu.make_async_copy(apo_hbm, rxi.at[1], ld_rx.at[1])
    l_sg = pltpu.make_async_copy(
        signs_hbm.at[pl.ds(pl.multiple_of(256 * tx, 256), 256)], sg, ld_sg
    )
    l_rx.start()
    l_ap.start()
    l_sg.start()
    for i in range(4):
        enc_load(i).start()

    def tx_load(i):
        return pltpu.make_async_copy(
            tx_hbm.at[:, pl.ds(pl.multiple_of(LG * (4 * i + x), LG), LG)],
            txi.at[i], ld_tx.at[i],
        )

    for i in range(16):
        tx_load(i).start()

    barrier = pltpu.get_barrier_semaphore()
    for to in (partner, right, left):
        pl.semaphore_signal(barrier, inc=1, device_id=to, device_id_type=MESH)

    def greet(i, c):
        ii = i + 1
        to = dev(x, (y + ii // 8) % 4, (z + ii % 8) % 8, co)
        pl.semaphore_signal(barrier, inc=1, device_id=to, device_id_type=MESH)
        return c

    lax.fori_loop(0, 31, greet, 0)

    l_rx.wait()
    l_ap.wait()

    def conv(i, c):
        rows = pl.ds(pl.multiple_of(64 * i, 64), 64)
        rxs[0, rows, :] = rxi[0, rows, :].astype(F32).astype(BF16)
        rxs[1, rows, :] = rxi[1, rows, :].astype(F32).astype(BF16)
        return c

    lax.fori_loop(0, 16, conv, 0)
    own = pl.ds(pl.multiple_of(64 * g, 64), 64)
    rxa[g, 0] = rxs[0, own, :]
    rxa[g, 1] = rxs[1, own, :]
    pl.semaphore_wait(barrier, 34)

    half = pl.ds(pl.multiple_of(32 * co, 32), 32)
    step = 2 * zl - 1

    def rx_copy(i, to_y, to_z):
        gt = to_y * 4 + to_z // 2
        return rcopy(
            rxs.at[:, pl.ds(pl.multiple_of(64 * gt + 32 * co, 32), 32), :],
            rxa.at[g, :, half, :],
            rx_s.at[i], rx_r.at[g], dev(x, to_y, to_z, co),
        )

    def rx_start(i, c):
        rx_copy(i, (y + i // 3) % 4, (z + step * (1 + i % 3) + 8) % 8).start()
        return c

    def rx_start_y(i, c):
        rx_copy(12 + i, (y + 1 + i) % 4, z).start()
        return c

    lax.fori_loop(0, 12, rx_start, 0)
    lax.fori_loop(0, 3, rx_start_y, 0)

    l_sg.wait()
    signs_t = sg[...].astype(F32).T.astype(BF16)
    for i in range(4):
        enc_load(i).wait()

        def widen(j, c, i=i):
            e = pl.multiple_of(64 * i + 16 * j, 16)
            v = encb[pl.ds(e, 16)].astype(F32).reshape(256, 512)
            for b in range(4):
                encf[b, pl.ds(pl.multiple_of(e * 16, 256), 256), :] = v[:, 128 * b : 128 * b + 128]
            return c

        lax.fori_loop(0, 4, widen, 0)

    def decode(r, c):
        v = jnp.concatenate(
            [encf[b, pl.ds(r, 256, stride=16), :] for b in range(4)], axis=1
        ).astype(BF16)
        d = lax.dot_general(
            signs_t, v, (((1,), (0,)), ((), ())), preferred_element_type=F32
        )
        for b in range(4):
            part[pl.ds(b * 16 + r, 64, stride=64), :] = d[:, b * 128 : (b + 1) * 128]
        return c

    lax.fori_loop(0, 16, decode, 0)

    def prow(t, h):
        return pl.ds(pl.multiple_of(1024 * t + 512 * h, 512), 512)

    def sw_copy(i):
        zz = (1 - zl) if i < 2 else zl
        return rcopy(
            part.at[prow(2 * zz + 1 - co, i % 2), :], rb.at[i],
            sw_s.at[i], sw_r.at[i], partner,
        )

    for i in range(4):
        sw_copy(i).start()

    def ze_copy(h):
        return rcopy(zs.at[h], zb.at[h], ze_s.at[h], ze_r.at[h], mate)

    for h in range(2):
        sw_copy(h).wait_recv()
        zs[h] = part[prow(2 * (1 - zl) + co, h), :] + rb[h]
        ze_copy(h).start()

    def fw_copy(gs):
        ref = rxa.at[gs, :, half, :]
        return rcopy(ref, ref, fw_s.at[gs], fw_r.at[gs], partner)

    def fw(i, c):
        gs = (g + 1 + i) % 16
        pltpu.make_async_copy(
            rxa.at[gs, :, half, :], rxa.at[gs, :, half, :], rx_r.at[gs]
        ).wait()
        fw_copy(gs).start()
        return c

    lax.fori_loop(0, 15, fw, 0)

    def xg_copy(i, slot, h, to):
        ref = da.at[slot, pl.ds(512 * h, 512), :]
        return rcopy(ref, ref, xg_s.at[i], xg_r.at[i], to)

    for h in range(2):
        sw_copy(2 + h).wait_recv()
        ze_copy(h).wait_recv()
        tot = part[prow(tx, h), :] + rb[2 + h] + zb[h]
        da[x, pl.ds(512 * h, 512), :] = (tot * (1.0 / 1024)).astype(BF16)
        xg_copy(h, x, h, right).start()
        xg_copy(2 + h, x, h, left).start()
    xg_copy(0, xl, 0, right).wait_recv()
    xg_copy(4, xl, 0, right).start()
    xg_copy(3, xr, 1, left).wait_recv()
    xg_copy(5, xr, 1, left).start()
    xg_copy(1, xl, 1, right).wait_recv()
    xg_copy(2, xr, 0, left).wait_recv()
    xg_copy(4, x, 0, right).wait_recv()
    xg_copy(5, x, 1, left).wait_recv()

    def fw_wait(i, c):
        gs = (g + 1 + i) % 16
        oth = rxa.at[gs, :, pl.ds(pl.multiple_of(32 * (1 - co), 32), 32), :]
        pltpu.make_async_copy(oth, oth, fw_r.at[gs]).wait()
        return c

    lax.fori_loop(0, 15, fw_wait, 0)
    for i in range(16):
        tx_load(i).wait()

    def flip(k, acc):
        rows = pl.ds(pl.multiple_of(64 * k, 64), 64)
        v = jnp.concatenate([da[i, rows, :] for i in range(4)], axis=0)
        t = v.astype(F32).T
        dt[pl.ds(pl.multiple_of(128 * k, 128), 128), :] = t.astype(BF16)
        return acc + t

    total = lax.fori_loop(0, 16, flip, jnp.zeros((128, 256), F32))
    hi = total.astype(BF16)
    sh[0:128, :] = hi
    sh[128:256, :] = (total - hi.astype(F32)).astype(BF16)

    def ci_copy(i):
        return rcopy(send.at[i], ib.at[i], ci_s.at[i], ci_r.at[i], partner)

    def y_copy(i):
        d = i // 4
        to = dev(x, (y + 1 + d) % 4, z, co)
        return rcopy(ys.at[i], yb.at[i], y_s.at[i], y_r.at[i], to)

    def finish(i):
        ci_copy(i).wait_recv()
        tot = keep[i] + ib[i]

        @pl.when(i < 12)
        def _():
            ys[i] = tot.astype(BF16)
            y_copy(i).start()

        @pl.when(i >= 12)
        def _():
            keep[i] = tot

    def block(i, c):
        gt = ((y + 1 + i // 4) % 4) * 4 + i % 4
        rxv = rxa[gt, 0].astype(F32)
        apv = rxa[gt, 1].astype(F32)
        v0 = jnp.where(rxv == 0.0, apv, 0.0)
        v1 = jnp.where(rxv == 1.0, apv, 0.0)
        v2 = jnp.where(rxv == 2.0, apv, 0.0)
        zero = jnp.zeros_like(v0)
        ws = (-v0, v0 - v1, v1 - v2, v2)
        bs = (v0, v1, v2, zero)

        def rows_of(parts):
            return jnp.concatenate(
                [parts[b][16 * i : 16 * i + 16] for i in range(4) for b in range(4)], axis=0
            ).astype(BF16)

        w = rows_of(ws)
        base = jnp.dot(sh[...], rows_of(bs), preferred_element_type=F32)
        delta[...] = jnp.dot(dt[...], w, preferred_element_type=F32)
        t = txi[gt].astype(F32)
        for q in range(4):
            acc = base[32 * q : 32 * q + 32] + base[128 + 32 * q : 160 + 32 * q]
            for k in range(16):
                acc = acc + t[k : k + 1] * delta[128 * k + 32 * q : 128 * k + 32 * q + 32, :]
            to_keep = (q % 2) == co

            @pl.when(to_keep)
            def _(acc=acc, q=q):
                keep[i, q // 2] = acc

            @pl.when(jnp.logical_not(to_keep))
            def _(acc=acc, q=q):
                send[i, q // 2] = acc

        ci_copy(i).start()

        @pl.when(i > 0)
        def _():
            finish(i - 1)

        return c

    lax.fori_loop(0, 16, block, 0)
    finish(15)

    def z_copy(d):
        zt = (z + d) % 8
        return rcopy(zss.at[zt], zrb.at[d - 1], z_s.at[d - 1], z_r.at[d - 1], dev(x, y, zt, co))

    def y_wait(i, c):
        y_copy(i).wait_recv()
        return c

    lax.fori_loop(0, 12, y_wait, 0)

    def ysum(h, c):
        for q in range(2):
            tot = keep[12 + h, q]
            for d in range(3):
                tot = tot + yb[4 * d + h, q].astype(F32)
            zss[2 * h + q] = tot
        return c

    lax.fori_loop(0, 4, ysum, 0)
    for d in range(1, 8):
        z_copy(d).start()
    for d in range(1, 8):
        z_copy(d).wait_recv()
    tot = zss[z]
    for d in range(7):
        tot = tot + zrb[d]
    out_ref[...] = (tot * 0.125).T

    for i in range(4):
        sw_copy(i).wait_send()
    for h in range(2):
        ze_copy(h).wait_send()

    def drain_rx(i, c):
        rx_copy(i, y, z).wait_send()
        fw_copy((g + 1 + i) % 16).wait_send()
        return c

    lax.fori_loop(0, 15, drain_rx, 0)
    for i, (slot, h, to) in enumerate(
        ((x, 0, right), (x, 1, right), (x, 0, left), (x, 1, left), (xl, 0, right), (xr, 1, left))
    ):
        xg_copy(i, slot, h, to).wait_send()

    def drain_ci(i, c):
        ci_copy(i).wait_send()
        return c

    lax.fori_loop(0, 16, drain_ci, 0)

    def drain_y(i, c):
        y_copy(i).wait_send()
        return c

    lax.fori_loop(0, 12, drain_y, 0)
    for d in range(1, 8):
        z_copy(d).wait_send()


def on_device(encoded, signs, tx_block, rx_block, apodization):
    dma = pltpu.SemaphoreType.DMA
    hbm = pl.BlockSpec(memory_space=pl.ANY)
    return pl.pallas_call(
        kernel,
        out_shape=jax.ShapeDtypeStruct((256, 32), F32),
        in_specs=[hbm] * 5,
        out_specs=pl.BlockSpec(memory_space=pltpu.VMEM),
        scratch_shapes=[
            pltpu.VMEM((256, 16, 512), BF16),
            pltpu.VMEM((4, 4096, 128), F32),
            pltpu.VMEM((256, 64), jnp.int32),
            pltpu.VMEM((4096, 128), F32),
            pltpu.VMEM((4, 512, 128), F32),
            pltpu.VMEM((2, 512, 128), F32),
            pltpu.VMEM((2, 512, 128), F32),
            pltpu.VMEM((4, 1024, 128), BF16),
            pltpu.VMEM((2048, 256), BF16),
            pltpu.VMEM((256, 256), BF16),
            pltpu.VMEM((2, 1024, 256), jnp.int32),
            pltpu.VMEM((2, 1024, 256), BF16),
            pltpu.VMEM((16, 2, 64, 256), BF16),
            pltpu.VMEM((16, 16, 256), jnp.int32),
            pltpu.VMEM((2048, 256), F32),
            pltpu.VMEM((16, 2, 32, 256), F32),
            pltpu.VMEM((16, 2, 32, 256), F32),
            pltpu.VMEM((16, 2, 32, 256), F32),
            pltpu.VMEM((12, 2, 32, 256), BF16),
            pltpu.VMEM((12, 2, 32, 256), BF16),
            pltpu.VMEM((8, 32, 256), F32),
            pltpu.VMEM((7, 32, 256), F32),
            dma((4,)), dma((2,)), dma, dma((16,)),
            dma((15,)), dma((16,)), dma((16,)), dma((16,)),
            dma((4,)), dma((4,)), dma((2,)), dma((2,)), dma((6,)), dma((6,)),
            dma((16,)), dma((16,)), dma((12,)), dma((12,)), dma((7,)), dma((7,)),
        ],
        compiler_params=pltpu.CompilerParams(
            collective_id=0, has_side_effects=True, vmem_limit_bytes=60 * 1024 * 1024
        ),
    )(encoded, signs, tx_block, rx_block, apodization)


def solution(mesh):
    placed = (P("tx", "img", None), P(), P("tx", None), P(None, "img"), P(None, "img"))
    return jax.shard_map(
        on_device, mesh=mesh, in_specs=placed, out_specs=P("img", "tx"), check_vma=False
    )
```

```python
import jax
import jax.numpy as jnp
from jax import lax
from jax.experimental import pallas as pl
from jax.experimental.pallas import tpu as pltpu
from jax.sharding import PartitionSpec as P

MESH = pl.DeviceIdType.MESH
F32 = jnp.float32
BF16 = jnp.bfloat16
LG = 256
NCH = 4
CH = 1024 // NCH
LAG = 3


def kernel(
    enc_hbm, signs_hbm, tx_hbm, rx_hbm, apo_hbm, out_ref,
    encb, encf, sg, part, rb, zs, zb, zsc, zbc, da, dt, sh, rxi, rxs, rxa, txi,
    delta, keep, send, ib, ys, yb, zss, zrb,
    ld_enc, ld_rx, ld_sg, ld_tx,
    rx_s, rx_r, fw_s, fw_r, sw_s, sw_r, ze_s, ze_r, zc_s, zc_r, xg_s, xg_r,
    ci_s, ci_r, y_s, y_r, z_s, z_r,
):
    tx = lax.axis_index("tx")
    img = lax.axis_index("img")
    zl = tx // 2
    co = tx % 2
    y = img // 16
    zh = (img // 4) % 4
    x = img % 4
    z = zh * 2 + zl
    g = y * 4 + zh

    def dev(xx, yy, zz, cc):
        return {"tx": (zz % 2) * 2 + cc, "img": (yy * 4 + zz // 2) * 4 + xx}

    partner = dev(x, y, z, 1 - co)
    mate = dev(x, y, zh * 2 + (1 - zl), co)
    xr = (x + 1) % 4
    xl = (x + 3) % 4
    right = dev(xr, y, z, co)
    left = dev(xl, y, z, co)

    def rcopy(src, dst, ss, rs, to):
        return pltpu.make_async_remote_copy(
            src_ref=src, dst_ref=dst, send_sem=ss, recv_sem=rs,
            device_id=to, device_id_type=MESH,
        )

    def enc_load(i):
        return pltpu.make_async_copy(
            enc_hbm.at[pl.ds(64 * i, 64)], encb.at[pl.ds(64 * i, 64)], ld_enc.at[i]
        )

    l_rx = pltpu.make_async_copy(rx_hbm, rxi.at[0], ld_rx.at[0])
    l_ap = pltpu.make_async_copy(apo_hbm, rxi.at[1], ld_rx.at[1])
    l_sg = pltpu.make_async_copy(
        signs_hbm.at[:, pl.ds(pl.multiple_of(256 * tx, 256), 256)], sg, ld_sg
    )
    l_rx.start()
    l_ap.start()
    l_sg.start()
    for i in range(4):
        enc_load(i).start()

    def tx_load(i):
        return pltpu.make_async_copy(
            tx_hbm.at[:, pl.ds(pl.multiple_of(LG * (4 * i + x), LG), LG)],
            txi.at[i], ld_tx.at[i],
        )

    for i in range(16):
        tx_load(i).start()

    barrier = pltpu.get_barrier_semaphore()
    for to in (partner, right, left):
        pl.semaphore_signal(barrier, inc=1, device_id=to, device_id_type=MESH)

    def greet(i, c):
        ii = i + 1
        to = dev(x, (y + ii // 8) % 4, (z + ii % 8) % 8, co)
        pl.semaphore_signal(barrier, inc=1, device_id=to, device_id_type=MESH)
        return c

    lax.fori_loop(0, 31, greet, 0)

    l_sg.wait()
    signs_t = sg[...].astype(F32).astype(BF16)
    for i in range(4):
        enc_load(i).wait()

        def widen(j, c, i=i):
            e = pl.multiple_of(64 * i + 16 * j, 16)
            v = encb[pl.ds(e, 16)].astype(F32)
            for h in range(2):
                w = v[:, 8 * h : 8 * h + 8].reshape(128, 512)
                for b in range(4):
                    encf[h, b, pl.ds(pl.multiple_of(e * 8, 128), 128), :] = w[
                        :, 128 * b : 128 * b + 128
                    ]
            return c

        lax.fori_loop(0, 4, widen, 0)

    def decode(r, c):
        v = jnp.concatenate(
            [encf[r // 8, b, pl.ds(r % 8, 256, stride=8), :] for b in range(4)], axis=1
        ).astype(BF16)
        d = lax.dot_general(
            signs_t, v, (((1,), (0,)), ((), ())), preferred_element_type=F32
        )
        for b in range(4):
            part[pl.ds(b * 16 + r, 64, stride=64), :] = d[:, b * 128 : (b + 1) * 128]
        return c

    lax.fori_loop(0, 16, decode, 0)

    l_rx.wait()
    l_ap.wait()

    def conv(i, c):
        rows = pl.ds(pl.multiple_of(64 * i, 64), 64)
        rxs[0, rows, :] = rxi[0, rows, :].astype(F32).astype(BF16)
        rxs[1, rows, :] = rxi[1, rows, :].astype(F32).astype(BF16)
        return c

    lax.fori_loop(0, 16, conv, 0)
    own = pl.ds(pl.multiple_of(64 * g, 64), 64)
    rxa[g, 0] = rxs[0, own, :]
    rxa[g, 1] = rxs[1, own, :]
    pl.semaphore_wait(barrier, 34)

    def prow(t, h):
        return pl.ds(pl.multiple_of(1024 * t + CH * h, CH), CH)

    def sw_copy(i):
        zz = (1 - zl) if i < NCH else zl
        return rcopy(
            part.at[prow(2 * zz + 1 - co, i % NCH), :], rb.at[i],
            sw_s.at[i], sw_r.at[i], partner,
        )

    for i in range(2 * NCH):
        sw_copy(i).start()

    half = pl.ds(pl.multiple_of(32 * co, 32), 32)
    step = 2 * zl - 1

    def rx_copy(i, to_y, to_z):
        gt = to_y * 4 + to_z // 2
        return rcopy(
            rxs.at[:, pl.ds(pl.multiple_of(64 * gt + 32 * co, 32), 32), :],
            rxa.at[g, :, half, :],
            rx_s.at[i], rx_r.at[g], dev(x, to_y, to_z, co),
        )

    def rx_start(i, c):
        rx_copy(i, (y + i // 3) % 4, (z + step * (1 + i % 3) + 8) % 8).start()
        return c

    def rx_start_y(i, c):
        rx_copy(12 + i, (y + 1 + i) % 4, z).start()
        return c

    def ze_copy(h):
        return rcopy(zs.at[h], zb.at[h], ze_s.at[h], ze_r.at[h], mate)

    def zc_copy(h):
        return rcopy(zsc.at[h], zbc.at[h], zc_s.at[h], zc_r.at[h], mate)

    for h in range(NCH):
        sw_copy(h).wait_recv()
        v = (part[prow(2 * (1 - zl) + co, h), :] + rb[h]).reshape(CH // 8, 8, 128)
        top = jnp.maximum(jnp.max(jnp.abs(v), axis=0), 1e-30)
        q = jnp.round(v * (32767.0 / top)[None]).astype(jnp.int32)
        zs[h] = q.reshape(CH, 128).astype(jnp.int16)
        zsc[h] = top * (1.0 / 32767.0)
        ze_copy(h).start()
        zc_copy(h).start()
        if h == 0:
            lax.fori_loop(0, 12, rx_start, 0)
            lax.fori_loop(0, 3, rx_start_y, 0)

    def xg_copy(i, slot, h, to):
        ref = da.at[slot, pl.ds(CH * h, CH), :]
        return rcopy(ref, ref, xg_s.at[i], xg_r.at[i], to)

    def relay(h):
        if h % 2 == 0:
            xg_copy(h, xl, h, right).wait_recv()
            xg_copy(2 * NCH + h, xl, h, right).start()
        else:
            xg_copy(NCH + h, xr, h, left).wait_recv()
            xg_copy(2 * NCH + h, xr, h, left).start()

    for h in range(NCH):
        sw_copy(NCH + h).wait_recv()
        ze_copy(h).wait_recv()
        zc_copy(h).wait_recv()
        v = zb[h].astype(jnp.int32).astype(F32).reshape(CH // 8, 8, 128) * zbc[h][None]
        tot = part[prow(tx, h), :] + rb[NCH + h] + v.reshape(CH, 128)
        da[x, pl.ds(CH * h, CH), :] = (tot * (1.0 / 1024)).astype(BF16)
        xg_copy(h, x, h, right).start()
        xg_copy(NCH + h, x, h, left).start()
        if h > 0:
            relay(h - 1)
    relay(NCH - 1)

    def fw_copy(gs):
        ref = rxa.at[gs, :, half, :]
        return rcopy(ref, ref, fw_s.at[gs], fw_r.at[gs], partner)

    def fw(i, c):
        gs = (g + 1 + i) % 16
        pltpu.make_async_copy(
            rxa.at[gs, :, half, :], rxa.at[gs, :, half, :], rx_r.at[gs]
        ).wait()
        fw_copy(gs).start()
        return c

    lax.fori_loop(0, 15, fw, 0)

    def flip(k, acc):
        rows = pl.ds(pl.multiple_of(64 * k, 64), 64)
        v = jnp.concatenate([da[i, rows, :] for i in range(4)], axis=0)
        t = v.astype(F32).T
        dt[pl.ds(pl.multiple_of(128 * k, 128), 128), :] = t.astype(BF16)
        return acc + t

    total = jnp.zeros((128, 256), F32)
    for h in range(NCH):
        if h % 2 == 0:
            xg_copy(NCH + h, xr, h, left).wait_recv()
        else:
            xg_copy(h, xl, h, right).wait_recv()
        xg_copy(2 * NCH + h, x, h, right).wait_recv()
        total = lax.fori_loop(h * (16 // NCH), (h + 1) * (16 // NCH), flip, total)
    hi = total.astype(BF16)
    sh[0:128, :] = hi
    sh[128:256, :] = (total - hi.astype(F32)).astype(BF16)

    def fw_wait(i, c):
        gs = (g + 1 + i) % 16
        oth = rxa.at[gs, :, pl.ds(pl.multiple_of(32 * (1 - co), 32), 32), :]
        pltpu.make_async_copy(oth, oth, fw_r.at[gs]).wait()
        return c

    lax.fori_loop(0, 15, fw_wait, 0)
    for i in range(16):
        tx_load(i).wait()

    def ci_copy(i):
        return rcopy(send.at[i], ib.at[i], ci_s.at[i], ci_r.at[i], partner)

    def y_copy(i):
        to = dev(x, (y + 1 + i % 4) % 4, z, co)
        return rcopy(ys.at[i], yb.at[i], y_s.at[i], y_r.at[i], to)

    def finish(i):
        ci_copy(i).wait_recv()
        tot = keep[i] + ib[i]

        @pl.when(i % 4 < 3)
        def _():
            ys[i] = tot.astype(BF16)
            y_copy(i).start()

        @pl.when(i % 4 == 3)
        def _():
            keep[i] = tot

    def z_copy(zt):
        d = (zt - z + 8) % 8 - 1
        return rcopy(zss.at[zt], zrb.at[d], z_s.at[d], z_r.at[d], dev(x, y, zt, co))

    def z_group(n):
        for d in range(3):
            y_copy(4 * n + d).wait_recv()
        for q in range(2):
            tot = keep[4 * n + 3, q]
            for d in range(3):
                tot = tot + yb[4 * n + d, q].astype(F32)
            zt = 2 * ((zh + 1 + n) % 4) + q
            zss[zt] = tot

            @pl.when(zt != z)
            def _(zt=zt):
                z_copy(zt).start()

    def block(i, c):
        gt = ((y + 1 + i % 4) % 4) * 4 + (zh + 1 + i // 4) % 4
        rxv = rxa[gt, 0].astype(F32)
        apv = rxa[gt, 1].astype(F32)
        v0 = jnp.where(rxv == 0.0, apv, 0.0)
        v1 = jnp.where(rxv == 1.0, apv, 0.0)
        v2 = jnp.where(rxv == 2.0, apv, 0.0)
        zero = jnp.zeros_like(v0)
        ws = (-v0, v0 - v1, v1 - v2, v2)
        bs = (v0, v1, v2, zero)

        def rows_of(parts):
            return jnp.concatenate(
                [parts[b][16 * i : 16 * i + 16] for i in range(4) for b in range(4)], axis=0
            ).astype(BF16)

        w = rows_of(ws)
        base = jnp.dot(sh[...], rows_of(bs), preferred_element_type=F32)
        delta[...] = jnp.dot(dt[...], w, preferred_element_type=F32)
        t = txi[gt].astype(F32)
        for q in range(4):
            acc = base[32 * q : 32 * q + 32] + base[128 + 32 * q : 160 + 32 * q]
            for k in range(16):
                acc = acc + t[k : k + 1] * delta[128 * k + 32 * q : 128 * k + 32 * q + 32, :]
            to_keep = (q % 2) == co

            @pl.when(to_keep)
            def _(acc=acc, q=q):
                keep[i, q // 2] = acc

            @pl.when(jnp.logical_not(to_keep))
            def _(acc=acc, q=q):
                send[i, q // 2] = acc

        ci_copy(i).start()

        @pl.when(i >= LAG)
        def _():
            finish(i - LAG)

        @pl.when(jnp.logical_and(i - LAG >= 7, (i - LAG) % 4 == 3))
        def _():
            z_group((i - LAG - 7) // 4)

        return c

    lax.fori_loop(0, 16, block, 0)
    for i in range(16 - LAG, 16):
        finish(i)
    z_group(2)
    z_group(3)
    for d in range(1, 8):
        z_copy((z + d) % 8).wait_recv()
    tot = zss[z]
    for d in range(7):
        tot = tot + zrb[d]
    out_ref[...] = tot * 0.125

    for i in range(2 * NCH):
        sw_copy(i).wait_send()
    for h in range(NCH):
        ze_copy(h).wait_send()
        zc_copy(h).wait_send()

    def drain_rx(i, c):
        rx_copy(i, y, z).wait_send()
        fw_copy((g + 1 + i) % 16).wait_send()
        return c

    lax.fori_loop(0, 15, drain_rx, 0)
    for i in range(3 * NCH):
        xg_copy(i, x, i % NCH, right).wait_send()

    def drain_ci(i, c):
        ci_copy(i).wait_send()

        @pl.when(i % 4 < 3)
        def _():
            y_copy(i).wait_send()

        return c

    lax.fori_loop(0, 16, drain_ci, 0)
    for d in range(1, 8):
        z_copy((z + d) % 8).wait_send()


def on_device(encoded, signs, tx_block, rx_block, apodization):
    dma = pltpu.SemaphoreType.DMA
    hbm = pl.BlockSpec(memory_space=pl.ANY)
    return pl.pallas_call(
        kernel,
        out_shape=jax.ShapeDtypeStruct((32, 256), F32),
        in_specs=[hbm] * 5,
        out_specs=pl.BlockSpec(memory_space=pltpu.VMEM),
        scratch_shapes=[
            pltpu.VMEM((256, 16, 512), BF16),
            pltpu.VMEM((2, 4, 2048, 128), F32),
            pltpu.VMEM((64, 256), jnp.int32),
            pltpu.VMEM((4096, 128), F32),
            pltpu.VMEM((2 * NCH, CH, 128), F32),
            pltpu.VMEM((NCH, CH, 128), jnp.int16),
            pltpu.VMEM((NCH, CH, 128), jnp.int16),
            pltpu.VMEM((NCH, 8, 128), F32),
            pltpu.VMEM((NCH, 8, 128), F32),
            pltpu.VMEM((4, 1024, 128), BF16),
            pltpu.VMEM((2048, 256), BF16),
            pltpu.VMEM((256, 256), BF16),
            pltpu.VMEM((2, 1024, 256), jnp.int32),
            pltpu.VMEM((2, 1024, 256), BF16),
            pltpu.VMEM((16, 2, 64, 256), BF16),
            pltpu.VMEM((16, 16, 256), jnp.int32),
            pltpu.VMEM((2048, 256), F32),
            pltpu.VMEM((16, 2, 32, 256), F32),
            pltpu.VMEM((16, 2, 32, 256), F32),
            pltpu.VMEM((16, 2, 32, 256), F32),
            pltpu.VMEM((16, 2, 32, 256), BF16),
            pltpu.VMEM((16, 2, 32, 256), BF16),
            pltpu.VMEM((8, 32, 256), F32),
            pltpu.VMEM((7, 32, 256), F32),
            dma((4,)), dma((2,)), dma, dma((16,)),
            dma((15,)), dma((16,)), dma((16,)), dma((16,)),
            dma((2 * NCH,)), dma((2 * NCH,)), dma((NCH,)), dma((NCH,)), dma((NCH,)), dma((NCH,)),
            dma((3 * NCH,)), dma((3 * NCH,)),
            dma((16,)), dma((16,)), dma((16,)), dma((16,)), dma((7,)), dma((7,)),
        ],
        compiler_params=pltpu.CompilerParams(
            collective_id=0, has_side_effects=True, vmem_limit_bytes=60 * 1024 * 1024
        ),
    )(encoded, signs.T, tx_block, rx_block, apodization).T


def solution(mesh):
    placed = (P("tx", "img", None), P(), P("tx", None), P(None, "img"), P(None, "img"))
    return jax.shard_map(
        on_device, mesh=mesh, in_specs=placed, out_specs=P("img", "tx"), check_vma=False
    )
```

```python
import jax
import jax.numpy as jnp
from jax import lax
from jax.experimental import pallas as pl
from jax.experimental.pallas import tpu as pltpu
from jax.sharding import PartitionSpec as P

MESH = pl.DeviceIdType.MESH
F32 = jnp.float32
BF16 = jnp.bfloat16
LG = 256
NCH = 4
CH = 1024 // NCH
LAG = 3
AHEAD = 4


def packed(table):
    word = sum(v << (2 * i) for i, v in enumerate(table))
    return word - (1 << 32) if word >> 31 else word


ORDER_Z = packed((1, 1, 1, 3, 3, 3, 0, 1, 2, 2, 2, 0, 0, 3, 2, 0))
ORDER_Y = packed((2, 1, 3, 2, 1, 3, 2, 0, 2, 1, 3, 1, 3, 0, 0, 0))


def kernel(
    enc_hbm, signs_hbm, tx_hbm, rx_hbm, apo_hbm, out_ref,
    encb, encf, sg, part, rb, zs, zb, zsc, zbc, da, dt, rxi, rxs, rxa, txi,
    delta, keep, send, ib, ys, yb, zss, zrb, zown,
    ld_enc, ld_rx, ld_sg, ld_tx,
    rx_s, rx_r, fw_s, fw_r, sw_s, sw_r, ze_s, ze_r, zc_s, zc_r, xg_s, xg_r,
    ci_s, ci_r, y_s, y_r, z_s, z_r, ready,
):
    tx = lax.axis_index("tx")
    img = lax.axis_index("img")
    zl = tx // 2
    co = tx % 2
    y = img // 16
    zh = (img // 4) % 4
    x = img % 4
    z = zh * 2 + zl
    g = y * 4 + zh

    def dev(xx, yy, zz, cc):
        return {"tx": (zz % 2) * 2 + cc, "img": (yy * 4 + zz // 2) * 4 + xx}

    partner = dev(x, y, z, 1 - co)
    mate = dev(x, y, zh * 2 + (1 - zl), co)
    xr = (x + 1) % 4
    xl = (x + 3) % 4
    right = dev(xr, y, z, co)
    left = dev(xl, y, z, co)
    across = dev((x + 2) % 4, y, z, co)

    def rcopy(src, dst, ss, rs, to):
        return pltpu.make_async_remote_copy(
            src_ref=src, dst_ref=dst, send_sem=ss, recv_sem=rs,
            device_id=to, device_id_type=MESH,
        )

    def enc_load(i):
        return pltpu.make_async_copy(
            enc_hbm.at[pl.ds(64 * i, 64)], encb.at[pl.ds(64 * i, 64)], ld_enc.at[i]
        )

    l_rx = pltpu.make_async_copy(rx_hbm, rxi.at[0], ld_rx.at[0])
    l_ap = pltpu.make_async_copy(apo_hbm, rxi.at[1], ld_rx.at[1])
    l_sg = pltpu.make_async_copy(
        signs_hbm.at[:, pl.ds(pl.multiple_of(256 * tx, 256), 256)], sg, ld_sg
    )
    l_sg.start()
    for i in range(4):
        enc_load(i).start()
    l_rx.start()
    l_ap.start()

    def tx_load(i):
        return pltpu.make_async_copy(
            tx_hbm.at[:, pl.ds(pl.multiple_of(LG * (4 * i + x), LG), LG)],
            txi.at[i], ld_tx.at[i],
        )

    for i in range(16):
        tx_load(i).start()

    barrier = pltpu.get_barrier_semaphore()
    for to in (partner, right, left, across):
        pl.semaphore_signal(barrier, inc=1, device_id=to, device_id_type=MESH)

    for d in range(1, 4):
        to = dev(x, (y + d) % 4, z, co)
        pl.semaphore_signal(barrier, inc=1, device_id=to, device_id_type=MESH)
    for d in range(1, 8):
        to = dev(x, y, (z + d) % 8, co)
        pl.semaphore_signal(barrier, inc=1, device_id=to, device_id_type=MESH)

    l_sg.wait()
    signs_t = sg[...].astype(F32).astype(BF16)
    for i in range(4):
        enc_load(i).wait()

        def widen(j, c, i=i):
            e = pl.multiple_of(64 * i + 16 * j, 16)
            v = encb[pl.ds(e, 16)].astype(F32)
            for h in range(2):
                w = v[:, 8 * h : 8 * h + 8].reshape(128, 512)
                for b in range(4):
                    encf[h, b, pl.ds(pl.multiple_of(e * 8, 128), 128), :] = w[
                        :, 128 * b : 128 * b + 128
                    ]
            return c

        lax.fori_loop(0, 4, widen, 0)

    def decode(r, c):
        v = jnp.concatenate(
            [encf[r // 8, b, pl.ds(r % 8, 256, stride=8), :] for b in range(4)], axis=1
        ).astype(BF16)
        d = lax.dot_general(
            signs_t, v, (((1,), (0,)), ((), ())), preferred_element_type=F32
        )
        for b in range(4):
            part[pl.ds(b * 16 + r, 64, stride=64), :] = d[:, b * 128 : (b + 1) * 128]
        return c

    lax.fori_loop(0, 16, decode, 0, unroll=4)

    l_rx.wait()
    l_ap.wait()

    def conv(i, c):
        rows = pl.ds(pl.multiple_of(64 * i, 64), 64)
        rxs[0, rows, :] = rxi[0, rows, :].astype(F32).astype(BF16)
        rxs[1, rows, :] = rxi[1, rows, :].astype(F32).astype(BF16)
        return c

    lax.fori_loop(0, 16, conv, 0)
    own = pl.ds(pl.multiple_of(64 * g, 64), 64)
    rxa[g, 0] = rxs[0, own, :]
    rxa[g, 1] = rxs[1, own, :]
    pl.semaphore_wait(barrier, 14)
    for d in range(1, 4):
        to = dev(x, (y + d) % 4, z, co)
        pl.semaphore_signal(ready, inc=1, device_id=to, device_id_type=MESH)

    def prow(t, h):
        return pl.ds(pl.multiple_of(1024 * t + CH * h, CH), CH)

    def sw_copy(i):
        zz = (1 - zl) if i < NCH else zl
        return rcopy(
            part.at[prow(2 * zz + 1 - co, i % NCH), :], rb.at[i],
            sw_s.at[i], sw_r.at[i], partner,
        )

    for i in range(2 * NCH):
        sw_copy(i).start()

    half = pl.ds(pl.multiple_of(32 * co, 32), 32)
    step = 2 * zl - 1

    def rx_copy(i, to_y, to_z):
        gt = to_y * 4 + to_z // 2
        return rcopy(
            rxs.at[:, pl.ds(pl.multiple_of(64 * gt + 32 * co, 32), 32), :],
            rxa.at[g, :, half, :],
            rx_s.at[i], rx_r.at[g], dev(x, to_y, to_z, co),
        )

    def rx_start(i, c):
        d = jnp.where(i < 8, 1 + i % 2, 3)
        yy = jnp.where(i < 8, i // 2, i - 8)
        rx_copy(i, (y + yy + 1) % 4, (z + step * d + 8) % 8).start()
        return c

    def rx_start_y(i, c):
        rx_copy(12 + i, (y + 1 + i) % 4, z).start()
        return c

    pl.semaphore_wait(ready, 3)
    lax.fori_loop(0, 8, rx_start, 0)
    lax.fori_loop(0, 3, rx_start_y, 0)
    lax.fori_loop(8, 12, rx_start, 0)

    def ze_copy(h):
        return rcopy(zs.at[h], zb.at[h], ze_s.at[h], ze_r.at[h], mate)

    def zc_copy(h):
        return rcopy(zsc.at[h], zbc.at[h], zc_s.at[h], zc_r.at[h], mate)

    for h in range(NCH):
        sw_copy(h).wait_recv()
        v = (part[prow(2 * (1 - zl) + co, h), :] + rb[h]).reshape(CH // 8, 8, 128)
        top = jnp.maximum(jnp.max(jnp.abs(v), axis=0), 1e-30)
        q = jnp.round(v * (32767.0 / top)[None]).astype(jnp.int32)
        zs[h] = q.reshape(CH, 128).astype(jnp.int16)
        zsc[h] = top * (1.0 / 32767.0)
        ze_copy(h).start()
        zc_copy(h).start()

    def xg_copy(i, slot, h, to):
        ref = da.at[slot, pl.ds(CH * h, CH), :]
        return rcopy(ref, ref, xg_s.at[i], xg_r.at[i], to)

    def relay(h):
        if h == NCH - 1:
            return
        if h == 0:
            xg_copy(h, xl, h, right).wait_recv()
            xg_copy(2 * NCH + h, xl, h, right).start()
        else:
            xg_copy(NCH + h, xr, h, left).wait_recv()
            xg_copy(2 * NCH + h, xr, h, left).start()

    for h in range(NCH):
        sw_copy(NCH + h).wait_recv()
        ze_copy(h).wait_recv()
        zc_copy(h).wait_recv()
        v = zb[h].astype(jnp.int32).astype(F32).reshape(CH // 8, 8, 128) * zbc[h][None]
        tot = part[prow(tx, h), :] + rb[NCH + h] + v.reshape(CH, 128)
        da[x, pl.ds(CH * h, CH), :] = (tot * (1.0 / 1024)).astype(BF16)
        if h == NCH - 1:
            xg_copy(2 * NCH + h, x, h, across).start()
        xg_copy(h, x, h, right).start()
        xg_copy(NCH + h, x, h, left).start()
        if h > 0:
            relay(h - 1)
    relay(NCH - 1)

    def dz_of(i):
        return (ORDER_Z >> (2 * i)) & 3

    def dy_of(i):
        return (ORDER_Y >> (2 * i)) & 3

    def gt_of(i):
        return ((y + dy_of(i)) % 4) * 4 + (zh + dz_of(i)) % 4

    def fw_copy(gs):
        ref = rxa.at[gs, :, half, :]
        return rcopy(ref, ref, fw_s.at[gs], fw_r.at[gs], partner)

    def fw(i):
        gs = gt_of(i)
        pltpu.make_async_copy(
            rxa.at[gs, :, half, :], rxa.at[gs, :, half, :], rx_r.at[gs]
        ).wait()
        fw_copy(gs).start()

    def fw_first(i, c):
        fw(i)
        return c

    lax.fori_loop(0, AHEAD, fw_first, 0)

    def flip(k, acc):
        rows = pl.ds(pl.multiple_of(64 * k, 64), 64)
        v = jnp.concatenate([da[i, rows, :] for i in range(4)], axis=0).astype(F32)
        dt[pl.ds(pl.multiple_of(128 * k, 128), 128), :] = v.T.astype(BF16)
        return acc + v

    total = jnp.zeros((256, 128), F32)
    for h in range(NCH):
        if h == 0 or h == NCH - 1:
            xg_copy(NCH + h, xr, h, left).wait_recv()
        if h > 0:
            xg_copy(h, xl, h, right).wait_recv()
        xg_copy(2 * NCH + h, x, h, right).wait_recv()
        total = lax.fori_loop(h * (16 // NCH), (h + 1) * (16 // NCH), flip, total)
    pieces = []
    for i in range(4):
        d0, d1, d2 = (total[64 * i + 16 * b : 64 * i + 16 * b + 16] for b in range(3))
        pieces += [-(d0 + d1), -d1, jnp.zeros_like(d2), d2]
    base_t = jnp.concatenate(pieces, axis=0).T
    hi = base_t.astype(BF16)
    dt[2048:2176, :] = hi
    dt[2176:2304, :] = (base_t - hi.astype(F32)).astype(BF16)

    def fw_wait(i):
        gs = gt_of(i)
        oth = rxa.at[gs, :, pl.ds(pl.multiple_of(32 * (1 - co), 32), 32), :]
        pltpu.make_async_copy(oth, oth, fw_r.at[gs]).wait()

    for i in range(16):
        tx_load(i).wait()

    def ci_copy(i):
        return rcopy(send.at[i], ib.at[i], ci_s.at[i], ci_r.at[i], partner)

    def slot_of(i):
        d = dy_of(i)
        return dz_of(i) * 3 + jnp.where(d == 2, 0, jnp.where(d == 1, 1, 2))

    def y_copy(m, d):
        to = dev(x, (y + d) % 4, z, co)
        return rcopy(ys.at[m], yb.at[m], y_s.at[m], y_r.at[m], to)

    def z_copy(zt):
        d = (zt - z + 8) % 8 - 1
        return rcopy(zss.at[zt], zrb.at[d], z_s.at[d], z_r.at[d], dev(x, y, zt, co))

    def finish(i):
        ci_copy(i).wait_recv()

        @pl.when(dy_of(i) != 0)
        def _():
            m = slot_of(i)
            ys[m] = (keep[i] + ib[i]).astype(BF16)
            y_copy(m, dy_of(i)).start()

        @pl.when(dy_of(i) == 0)
        def _():
            n = dz_of(i)
            for d in range(3):
                y_copy(3 * n + d, 1).wait_recv()
            for q in range(2):
                tot = keep[i, q] + ib[i, q]
                for d in range(3):
                    tot = tot + yb[3 * n + d, q].astype(F32)
                zt = 2 * ((zh + n) % 4) + q
                zss[zt] = tot.astype(BF16)

                @pl.when(zt != z)
                def _(zt=zt):
                    z_copy(zt).start()

                @pl.when(zt == z)
                def _(tot=tot):
                    zown[...] = tot

    def block(i, c):
        gt = gt_of(i)

        @pl.when(i + AHEAD < 15)
        def _():
            fw(i + AHEAD)

        @pl.when(i < 15)
        def _():
            fw_wait(i)

        rxv = rxa[gt, 0].astype(F32)
        apv = rxa[gt, 1].astype(F32)
        v0 = jnp.where(rxv == 0.0, apv, 0.0)
        v1 = jnp.where(rxv == 1.0, apv, 0.0)
        v2 = jnp.where(rxv == 2.0, apv, 0.0)
        ws = (-v0, v0 - v1, v1 - v2, v2)
        w = jnp.concatenate(
            [ws[b][16 * i4 : 16 * i4 + 16] for i4 in range(4) for b in range(4)], axis=0
        ).astype(BF16)
        delta[...] = jnp.dot(dt[...], w, preferred_element_type=F32)
        t = txi[gt].astype(F32)
        for q in range(4):
            acc = (
                delta[2048 + 32 * q : 2080 + 32 * q, :] + delta[2176 + 32 * q : 2208 + 32 * q, :]
            )
            for k in range(16):
                acc = acc + t[k : k + 1] * delta[128 * k + 32 * q : 128 * k + 32 * q + 32, :]
            to_keep = (q % 2) == co

            @pl.when(to_keep)
            def _(acc=acc, q=q):
                keep[i, q // 2] = acc

            @pl.when(jnp.logical_not(to_keep))
            def _(acc=acc, q=q):
                send[i, q // 2] = acc

        ci_copy(i).start()

        @pl.when(i >= LAG)
        def _():
            finish(i - LAG)

        return c

    lax.fori_loop(0, 16, block, 0)
    for i in range(16 - LAG, 16):
        finish(i)

    for i in range(2 * NCH):
        sw_copy(i).wait_send()
    for h in range(NCH):
        ze_copy(h).wait_send()
        zc_copy(h).wait_send()

    def drain_rx(i, c):
        rx_copy(i, y, z).wait_send()
        fw_copy(gt_of(i)).wait_send()
        return c

    lax.fori_loop(0, 15, drain_rx, 0)
    for i in range(3 * NCH):
        xg_copy(i, x, i % NCH, right).wait_send()

    def drain_ci(i, c):
        ci_copy(i).wait_send()
        return c

    lax.fori_loop(0, 16, drain_ci, 0)

    def drain_y(i, c):
        y_copy(i, 1).wait_send()
        return c

    lax.fori_loop(0, 12, drain_y, 0)
    for d in range(1, 8):
        z_copy((z + d) % 8).wait_send()

    for d in range(1, 8):
        z_copy((z + d) % 8).wait_recv()
    tot = zown[...]
    for d in range(7):
        tot = tot + zrb[d].astype(F32)
    out_ref[...] = tot * 0.125


def on_device(encoded, signs, tx_block, rx_block, apodization):
    dma = pltpu.SemaphoreType.DMA
    hbm = pl.BlockSpec(memory_space=pl.ANY)
    return pl.pallas_call(
        kernel,
        out_shape=jax.ShapeDtypeStruct((32, 256), F32),
        in_specs=[hbm] * 5,
        out_specs=pl.BlockSpec(memory_space=pltpu.VMEM),
        scratch_shapes=[
            pltpu.VMEM((256, 16, 512), BF16),
            pltpu.VMEM((2, 4, 2048, 128), F32),
            pltpu.VMEM((64, 256), jnp.int32),
            pltpu.VMEM((4096, 128), F32),
            pltpu.VMEM((2 * NCH, CH, 128), F32),
            pltpu.VMEM((NCH, CH, 128), jnp.int16),
            pltpu.VMEM((NCH, CH, 128), jnp.int16),
            pltpu.VMEM((NCH, 8, 128), F32),
            pltpu.VMEM((NCH, 8, 128), F32),
            pltpu.VMEM((4, 1024, 128), BF16),
            pltpu.VMEM((2304, 256), BF16),
            pltpu.VMEM((2, 1024, 256), jnp.int32),
            pltpu.VMEM((2, 1024, 256), BF16),
            pltpu.VMEM((16, 2, 64, 256), BF16),
            pltpu.VMEM((16, 16, 256), jnp.int32),
            pltpu.VMEM((2304, 256), F32),
            pltpu.VMEM((16, 2, 32, 256), F32),
            pltpu.VMEM((16, 2, 32, 256), F32),
            pltpu.VMEM((16, 2, 32, 256), F32),
            pltpu.VMEM((12, 2, 32, 256), BF16),
            pltpu.VMEM((12, 2, 32, 256), BF16),
            pltpu.VMEM((8, 32, 256), BF16),
            pltpu.VMEM((7, 32, 256), BF16),
            pltpu.VMEM((32, 256), F32),
            dma((4,)), dma((2,)), dma, dma((16,)),
            dma((15,)), dma((16,)), dma((16,)), dma((16,)),
            dma((2 * NCH,)), dma((2 * NCH,)), dma((NCH,)), dma((NCH,)), dma((NCH,)), dma((NCH,)),
            dma((3 * NCH,)), dma((3 * NCH,)),
            dma((16,)), dma((16,)), dma((12,)), dma((12,)), dma((7,)), dma((7,)), pltpu.SemaphoreType.REGULAR,
        ],
        compiler_params=pltpu.CompilerParams(
            collective_id=0, has_side_effects=True, vmem_limit_bytes=60 * 1024 * 1024
        ),
    )(encoded, signs.T, tx_block, rx_block, apodization).T


def solution(mesh):
    placed = (P("tx", "img", None), P(), P("tx", None), P(None, "img"), P(None, "img"))
    return jax.shard_map(
        on_device, mesh=mesh, in_specs=placed, out_specs=P("img", "tx"), check_vma=False
    )
```

```python
import jax
import jax.numpy as jnp
from jax import lax
from jax.experimental import pallas as pl
from jax.experimental.pallas import tpu as pltpu
from jax.sharding import PartitionSpec as P

MESH = pl.DeviceIdType.MESH
F32 = jnp.float32
BF16 = jnp.bfloat16
LG = 256
NCH = 4
CH = 1024 // NCH
LAG = 3
AHEAD = 4


def packed(table):
    word = sum(v << (2 * i) for i, v in enumerate(table))
    return word - (1 << 32) if word >> 31 else word


ORDER_Z = packed((1, 1, 1, 0, 2, 2, 2, 1, 3, 3, 3, 2, 0, 0, 3, 0))
ORDER_Y = packed((2, 1, 3, 2, 2, 1, 3, 0, 2, 1, 3, 0, 1, 3, 0, 0))


def kernel(
    enc_hbm, signs_hbm, tx_hbm, rx_hbm, apo_hbm, out_ref,
    encb, encf, sg, part, rb, zs, zb, zsc, zbc, da, dt, rxi, rxs, rxa, txi,
    delta, keep, send, ib, ys, yb, zss, zrb, zown,
    ld_enc, ld_rx, ld_sg, ld_tx,
    rx_s, rx_r, fw_s, fw_r, sw_s, sw_r, ze_s, ze_r, zc_s, zc_r, xg_s, xg_r,
    ci_s, ci_r, y_s, y_r, z_s, z_r, ready,
):
    tx = lax.axis_index("tx")
    img = lax.axis_index("img")
    zl = tx // 2
    co = tx % 2
    y = img // 16
    zh = (img // 4) % 4
    x = img % 4
    z = zh * 2 + zl
    g = y * 4 + zh

    def dev(xx, yy, zz, cc):
        return {"tx": (zz % 2) * 2 + cc, "img": (yy * 4 + zz // 2) * 4 + xx}

    partner = dev(x, y, z, 1 - co)
    mate = dev(x, y, zh * 2 + (1 - zl), co)
    xr = (x + 1) % 4
    xl = (x + 3) % 4
    right = dev(xr, y, z, co)
    left = dev(xl, y, z, co)
    across = dev((x + 2) % 4, y, z, co)

    def rcopy(src, dst, ss, rs, to):
        return pltpu.make_async_remote_copy(
            src_ref=src, dst_ref=dst, send_sem=ss, recv_sem=rs,
            device_id=to, device_id_type=MESH,
        )

    def enc_load(i):
        return pltpu.make_async_copy(
            enc_hbm.at[pl.ds(64 * i, 64)], encb.at[pl.ds(64 * i, 64)], ld_enc.at[i]
        )

    l_rx = pltpu.make_async_copy(rx_hbm, rxi.at[0], ld_rx.at[0])
    l_ap = pltpu.make_async_copy(apo_hbm, rxi.at[1], ld_rx.at[1])
    l_sg = pltpu.make_async_copy(
        signs_hbm.at[:, pl.ds(pl.multiple_of(256 * tx, 256), 256)], sg, ld_sg
    )
    l_sg.start()
    for i in range(4):
        enc_load(i).start()
    l_rx.start()
    l_ap.start()

    def tx_load(i):
        return pltpu.make_async_copy(
            tx_hbm.at[:, pl.ds(pl.multiple_of(LG * (4 * i + x), LG), LG)],
            txi.at[i], ld_tx.at[i],
        )

    for i in range(16):
        tx_load(i).start()

    barrier = pltpu.get_barrier_semaphore()
    for to in (partner, right, left, across):
        pl.semaphore_signal(barrier, inc=1, device_id=to, device_id_type=MESH)

    for d in range(1, 4):
        to = dev(x, (y + d) % 4, z, co)
        pl.semaphore_signal(barrier, inc=1, device_id=to, device_id_type=MESH)
    for d in range(1, 8):
        to = dev(x, y, (z + d) % 8, co)
        pl.semaphore_signal(barrier, inc=1, device_id=to, device_id_type=MESH)

    l_sg.wait()
    signs_t = sg[...].astype(F32).astype(BF16)
    for i in range(4):
        enc_load(i).wait()

        def widen(j, c, i=i):
            e = pl.multiple_of(64 * i + 16 * j, 16)
            v = encb[pl.ds(e, 16)].astype(F32)
            for h in range(2):
                w = v[:, 8 * h : 8 * h + 8].reshape(128, 512)
                for b in range(4):
                    encf[h, b, pl.ds(pl.multiple_of(e * 8, 128), 128), :] = w[
                        :, 128 * b : 128 * b + 128
                    ]
            return c

        lax.fori_loop(0, 4, widen, 0)

    def decode(r, c):
        v = jnp.concatenate(
            [encf[r // 8, b, pl.ds(r % 8, 256, stride=8), :] for b in range(4)], axis=1
        ).astype(BF16)
        d = lax.dot_general(
            signs_t, v, (((1,), (0,)), ((), ())), preferred_element_type=F32
        )
        for b in range(4):
            part[pl.ds(b * 16 + r, 64, stride=64), :] = d[:, b * 128 : (b + 1) * 128]
        return c

    lax.fori_loop(0, 16, decode, 0, unroll=4)

    l_rx.wait()
    l_ap.wait()

    def conv(i, c):
        rows = pl.ds(pl.multiple_of(64 * i, 64), 64)
        rxs[0, rows, :] = rxi[0, rows, :].astype(F32).astype(BF16)
        rxs[1, rows, :] = rxi[1, rows, :].astype(F32).astype(BF16)
        return c

    lax.fori_loop(0, 16, conv, 0)
    own = pl.ds(pl.multiple_of(64 * g, 64), 64)
    rxa[g, 0] = rxs[0, own, :]
    rxa[g, 1] = rxs[1, own, :]
    pl.semaphore_wait(barrier, 14)
    for d in range(1, 4):
        to = dev(x, (y + d) % 4, z, co)
        pl.semaphore_signal(ready, inc=1, device_id=to, device_id_type=MESH)

    def prow(t, h):
        return pl.ds(pl.multiple_of(1024 * t + CH * h, CH), CH)

    def sw_copy(i):
        zz = (1 - zl) if i < NCH else zl
        return rcopy(
            part.at[prow(2 * zz + 1 - co, i % NCH), :], rb.at[i],
            sw_s.at[i], sw_r.at[i], partner,
        )

    for i in range(2 * NCH):
        sw_copy(i).start()

    half = pl.ds(pl.multiple_of(32 * co, 32), 32)
    step = 2 * zl - 1

    def rx_copy(i, to_y, to_z):
        gt = to_y * 4 + to_z // 2
        return rcopy(
            rxs.at[:, pl.ds(pl.multiple_of(64 * gt + 32 * co, 32), 32), :],
            rxa.at[g, :, half, :],
            rx_s.at[i], rx_r.at[g], dev(x, to_y, to_z, co),
        )

    def rx_start(i, c):
        d = jnp.where(i < 8, 1 + i % 2, 3)
        yy = jnp.where(i < 8, i // 2, i - 8)
        rx_copy(i, (y + yy + 1) % 4, (z + step * d + 8) % 8).start()
        return c

    def rx_start_y(i, c):
        rx_copy(12 + i, (y + 1 + i) % 4, z).start()
        return c

    pl.semaphore_wait(ready, 3)
    lax.fori_loop(0, 8, rx_start, 0)
    lax.fori_loop(0, 3, rx_start_y, 0)
    lax.fori_loop(8, 12, rx_start, 0)

    def ze_copy(h):
        return rcopy(zs.at[h], zb.at[h], ze_s.at[h], ze_r.at[h], mate)

    def zc_copy(h):
        return rcopy(zsc.at[h], zbc.at[h], zc_s.at[h], zc_r.at[h], mate)

    for h in range(NCH):
        sw_copy(h).wait_recv()
        v = (part[prow(2 * (1 - zl) + co, h), :] + rb[h]).reshape(CH // 8, 8, 128)
        top = jnp.maximum(jnp.max(jnp.abs(v), axis=0), 1e-30)
        q = jnp.round(v * (32767.0 / top)[None]).astype(jnp.int32)
        zs[h] = q.reshape(CH, 128).astype(jnp.int16)
        zsc[h] = top * (1.0 / 32767.0)
        ze_copy(h).start()
        zc_copy(h).start()

    def xg_copy(i, slot, h, to):
        ref = da.at[slot, pl.ds(CH * h, CH), :]
        return rcopy(ref, ref, xg_s.at[i], xg_r.at[i], to)

    def relay(h):
        if h == NCH - 1:
            return
        if h == 0:
            xg_copy(h, xl, h, right).wait_recv()
            xg_copy(2 * NCH + h, xl, h, right).start()
        else:
            xg_copy(NCH + h, xr, h, left).wait_recv()
            xg_copy(2 * NCH + h, xr, h, left).start()

    for h in range(NCH):
        sw_copy(NCH + h).wait_recv()
        ze_copy(h).wait_recv()
        zc_copy(h).wait_recv()
        v = zb[h].astype(jnp.int32).astype(F32).reshape(CH // 8, 8, 128) * zbc[h][None]
        tot = part[prow(tx, h), :] + rb[NCH + h] + v.reshape(CH, 128)
        da[x, pl.ds(CH * h, CH), :] = (tot * (1.0 / 1024)).astype(BF16)
        if h == NCH - 1:
            xg_copy(2 * NCH + h, x, h, across).start()
        xg_copy(h, x, h, right).start()
        xg_copy(NCH + h, x, h, left).start()
        if h > 0:
            relay(h - 1)
    relay(NCH - 1)

    def dz_of(i):
        return (ORDER_Z >> (2 * i)) & 3

    def dy_of(i):
        return (ORDER_Y >> (2 * i)) & 3

    def gt_of(i):
        return ((y + dy_of(i)) % 4) * 4 + (zh + dz_of(i)) % 4

    def fw_copy(gs):
        ref = rxa.at[gs, :, half, :]
        return rcopy(ref, ref, fw_s.at[gs], fw_r.at[gs], partner)

    def fw(i):
        gs = gt_of(i)
        pltpu.make_async_copy(
            rxa.at[gs, :, half, :], rxa.at[gs, :, half, :], rx_r.at[gs]
        ).wait()
        fw_copy(gs).start()

    def fw_first(i, c):
        fw(i)
        return c

    lax.fori_loop(0, AHEAD, fw_first, 0)

    def flip(k, acc):
        rows = pl.ds(pl.multiple_of(64 * k, 64), 64)
        v = jnp.concatenate([da[i, rows, :] for i in range(4)], axis=0).astype(F32)
        dt[pl.ds(pl.multiple_of(128 * k, 128), 128), :] = v.T.astype(BF16)
        return acc + v

    total = jnp.zeros((256, 128), F32)
    for h in range(NCH):
        if h == 0 or h == NCH - 1:
            xg_copy(NCH + h, xr, h, left).wait_recv()
        if h > 0:
            xg_copy(h, xl, h, right).wait_recv()
        xg_copy(2 * NCH + h, x, h, right).wait_recv()
        total = lax.fori_loop(h * (16 // NCH), (h + 1) * (16 // NCH), flip, total)
    pieces = []
    for i in range(4):
        d0, d1, d2 = (total[64 * i + 16 * b : 64 * i + 16 * b + 16] for b in range(3))
        pieces += [-(d0 + d1), -d1, jnp.zeros_like(d2), d2]
    base_t = jnp.concatenate(pieces, axis=0).T
    hi = base_t.astype(BF16)
    dt[2048:2176, :] = hi
    dt[2176:2304, :] = (base_t - hi.astype(F32)).astype(BF16)

    def fw_wait(i):
        gs = gt_of(i)
        oth = rxa.at[gs, :, pl.ds(pl.multiple_of(32 * (1 - co), 32), 32), :]
        pltpu.make_async_copy(oth, oth, fw_r.at[gs]).wait()

    for i in range(16):
        tx_load(i).wait()

    def ci_copy(i):
        return rcopy(send.at[i], ib.at[i], ci_s.at[i], ci_r.at[i], partner)

    def slot_of(i):
        d = dy_of(i)
        return dz_of(i) * 3 + jnp.where(d == 2, 0, jnp.where(d == 1, 1, 2))

    def y_copy(m, d):
        to = dev(x, (y + d) % 4, z, co)
        return rcopy(ys.at[m], yb.at[m], y_s.at[m], y_r.at[m], to)

    def z_copy(zt):
        d = (zt - z + 8) % 8 - 1
        return rcopy(zss.at[zt], zrb.at[d], z_s.at[d], z_r.at[d], dev(x, y, zt, co))

    def finish(i):
        ci_copy(i).wait_recv()

        @pl.when(dy_of(i) != 0)
        def _():
            m = slot_of(i)
            ys[m] = (keep[i] + ib[i]).astype(BF16)
            y_copy(m, dy_of(i)).start()

        @pl.when(dy_of(i) == 0)
        def _():
            n = dz_of(i)
            for d in range(3):
                y_copy(3 * n + d, 1).wait_recv()
            for q in range(2):
                tot = keep[i, q] + ib[i, q]
                for d in range(3):
                    tot = tot + yb[3 * n + d, q].astype(F32)
                zt = 2 * ((zh + n) % 4) + q
                zss[zt] = tot.astype(BF16)

                @pl.when(zt != z)
                def _(zt=zt):
                    z_copy(zt).start()

                @pl.when(zt == z)
                def _(tot=tot):
                    zown[...] = tot

    def block(i, c):
        gt = gt_of(i)

        @pl.when(i + AHEAD < 15)
        def _():
            fw(i + AHEAD)

        @pl.when(i < 15)
        def _():
            fw_wait(i)

        rxv = rxa[gt, 0].astype(F32)
        apv = rxa[gt, 1].astype(F32)
        v0 = jnp.where(rxv == 0.0, apv, 0.0)
        v1 = jnp.where(rxv == 1.0, apv, 0.0)
        v2 = jnp.where(rxv == 2.0, apv, 0.0)
        ws = (-v0, v0 - v1, v1 - v2, v2)
        w = jnp.concatenate(
            [ws[b][16 * i4 : 16 * i4 + 16] for i4 in range(4) for b in range(4)], axis=0
        ).astype(BF16)
        delta[...] = jnp.dot(dt[...], w, preferred_element_type=F32)
        t = txi[gt].astype(F32)
        for q in range(4):
            acc = (
                delta[2048 + 32 * q : 2080 + 32 * q, :] + delta[2176 + 32 * q : 2208 + 32 * q, :]
            )
            for k in range(16):
                acc = acc + t[k : k + 1] * delta[128 * k + 32 * q : 128 * k + 32 * q + 32, :]
            to_keep = (q % 2) == co

            @pl.when(to_keep)
            def _(acc=acc, q=q):
                keep[i, q // 2] = acc

            @pl.when(jnp.logical_not(to_keep))
            def _(acc=acc, q=q):
                send[i, q // 2] = acc

        ci_copy(i).start()

        @pl.when(i >= LAG)
        def _():
            finish(i - LAG)

        return c

    lax.fori_loop(0, 16, block, 0)
    for i in range(16 - LAG, 16):
        finish(i)

    for i in range(2 * NCH):
        sw_copy(i).wait_send()
    for h in range(NCH):
        ze_copy(h).wait_send()
        zc_copy(h).wait_send()

    def drain_rx(i, c):
        rx_copy(i, y, z).wait_send()
        fw_copy(gt_of(i)).wait_send()
        return c

    lax.fori_loop(0, 15, drain_rx, 0)
    for i in range(3 * NCH):
        xg_copy(i, x, i % NCH, right).wait_send()

    def drain_ci(i, c):
        ci_copy(i).wait_send()
        return c

    lax.fori_loop(0, 16, drain_ci, 0)

    def drain_y(i, c):
        y_copy(i, 1).wait_send()
        return c

    lax.fori_loop(0, 12, drain_y, 0)
    for d in range(1, 8):
        z_copy((z + d) % 8).wait_send()

    for d in range(1, 8):
        z_copy((z + d) % 8).wait_recv()
    tot = zown[...]
    for d in range(7):
        tot = tot + zrb[d].astype(F32)
    out_ref[...] = tot * 0.125


def on_device(encoded, signs, tx_block, rx_block, apodization):
    dma = pltpu.SemaphoreType.DMA
    hbm = pl.BlockSpec(memory_space=pl.ANY)
    return pl.pallas_call(
        kernel,
        out_shape=jax.ShapeDtypeStruct((32, 256), F32),
        in_specs=[hbm] * 5,
        out_specs=pl.BlockSpec(memory_space=pltpu.VMEM),
        scratch_shapes=[
            pltpu.VMEM((256, 16, 512), BF16),
            pltpu.VMEM((2, 4, 2048, 128), F32),
            pltpu.VMEM((64, 256), jnp.int32),
            pltpu.VMEM((4096, 128), F32),
            pltpu.VMEM((2 * NCH, CH, 128), F32),
            pltpu.VMEM((NCH, CH, 128), jnp.int16),
            pltpu.VMEM((NCH, CH, 128), jnp.int16),
            pltpu.VMEM((NCH, 8, 128), F32),
            pltpu.VMEM((NCH, 8, 128), F32),
            pltpu.VMEM((4, 1024, 128), BF16),
            pltpu.VMEM((2304, 256), BF16),
            pltpu.VMEM((2, 1024, 256), jnp.int32),
            pltpu.VMEM((2, 1024, 256), BF16),
            pltpu.VMEM((16, 2, 64, 256), BF16),
            pltpu.VMEM((16, 16, 256), jnp.int32),
            pltpu.VMEM((2304, 256), F32),
            pltpu.VMEM((16, 2, 32, 256), F32),
            pltpu.VMEM((16, 2, 32, 256), F32),
            pltpu.VMEM((16, 2, 32, 256), F32),
            pltpu.VMEM((12, 2, 32, 256), BF16),
            pltpu.VMEM((12, 2, 32, 256), BF16),
            pltpu.VMEM((8, 32, 256), BF16),
            pltpu.VMEM((7, 32, 256), BF16),
            pltpu.VMEM((32, 256), F32),
            dma((4,)), dma((2,)), dma, dma((16,)),
            dma((15,)), dma((16,)), dma((16,)), dma((16,)),
            dma((2 * NCH,)), dma((2 * NCH,)), dma((NCH,)), dma((NCH,)), dma((NCH,)), dma((NCH,)),
            dma((3 * NCH,)), dma((3 * NCH,)),
            dma((16,)), dma((16,)), dma((12,)), dma((12,)), dma((7,)), dma((7,)), pltpu.SemaphoreType.REGULAR,
        ],
        compiler_params=pltpu.CompilerParams(
            collective_id=0, has_side_effects=True, vmem_limit_bytes=60 * 1024 * 1024
        ),
    )(encoded, signs.T, tx_block, rx_block, apodization).T


def solution(mesh):
    placed = (P("tx", "img", None), P(), P("tx", None), P(None, "img"), P(None, "img"))
    return jax.shard_map(
        on_device, mesh=mesh, in_specs=placed, out_specs=P("img", "tx"), check_vma=False
    )
```

```python
import jax
import jax.numpy as jnp
from jax import lax
from jax.experimental import pallas as pl
from jax.experimental.pallas import tpu as pltpu
from jax.sharding import PartitionSpec as P

MESH = pl.DeviceIdType.MESH
F32 = jnp.float32
BF16 = jnp.bfloat16
LG = 256
NCH = 4
CH = 1024 // NCH
LAG = 3
AHEAD = 4


def packed(table):
    word = sum(v << (2 * i) for i, v in enumerate(table))
    return word - (1 << 32) if word >> 31 else word


ORDER_Z = packed((1,1,1,2,2,2,3,3,3,1,0,0,0,2,3,0))
ORDER_Y = packed((2,1,3,2,1,3,2,1,3,0,2,1,3,0,0,0))


def kernel(
    enc_hbm, signs_hbm, tx_hbm, rx_hbm, apo_hbm, out_ref,
    encb, encf, sg, part, rb, zs, zb, zsc, zbc, da, dt, rxi, rxs, rxa, txi,
    delta, keep, send, ib, ys, yb, zss, zrb, zown,
    ld_enc, ld_rx, ld_sg, ld_tx,
    rx_s, rx_r, fw_s, fw_r, sw_s, sw_r, ze_s, ze_r, zc_s, zc_r, xg_s, xg_r,
    ci_s, ci_r, y_s, y_r, z_s, z_r, ready,
):
    tx = lax.axis_index("tx")
    img = lax.axis_index("img")
    zl = tx // 2
    co = tx % 2
    y = img // 16
    zh = (img // 4) % 4
    x = img % 4
    z = zh * 2 + zl
    g = y * 4 + zh

    def dev(xx, yy, zz, cc):
        return {"tx": (zz % 2) * 2 + cc, "img": (yy * 4 + zz // 2) * 4 + xx}

    partner = dev(x, y, z, 1 - co)
    mate = dev(x, y, zh * 2 + (1 - zl), co)
    xr = (x + 1) % 4
    xl = (x + 3) % 4
    right = dev(xr, y, z, co)
    left = dev(xl, y, z, co)
    across = dev((x + 2) % 4, y, z, co)

    def rcopy(src, dst, ss, rs, to):
        return pltpu.make_async_remote_copy(
            src_ref=src, dst_ref=dst, send_sem=ss, recv_sem=rs,
            device_id=to, device_id_type=MESH,
        )

    def enc_load(i):
        return pltpu.make_async_copy(
            enc_hbm.at[pl.ds(64 * i, 64)], encb.at[pl.ds(64 * i, 64)], ld_enc.at[i]
        )

    l_rx = pltpu.make_async_copy(rx_hbm, rxi.at[0], ld_rx.at[0])
    l_ap = pltpu.make_async_copy(apo_hbm, rxi.at[1], ld_rx.at[1])
    l_sg = pltpu.make_async_copy(
        signs_hbm.at[:, pl.ds(pl.multiple_of(256 * tx, 256), 256)], sg, ld_sg
    )
    l_sg.start()
    for i in range(4):
        enc_load(i).start()
    l_rx.start()
    l_ap.start()

    def tx_load(i):
        return pltpu.make_async_copy(
            tx_hbm.at[:, pl.ds(pl.multiple_of(LG * (4 * i + x), LG), LG)],
            txi.at[i], ld_tx.at[i],
        )

    for i in range(16):
        tx_load(i).start()

    barrier = pltpu.get_barrier_semaphore()
    for to in (partner, right, left, across):
        pl.semaphore_signal(barrier, inc=1, device_id=to, device_id_type=MESH)

    for d in range(1, 4):
        to = dev(x, (y + d) % 4, z, co)
        pl.semaphore_signal(barrier, inc=1, device_id=to, device_id_type=MESH)
    for d in range(1, 8):
        to = dev(x, y, (z + d) % 8, co)
        pl.semaphore_signal(barrier, inc=1, device_id=to, device_id_type=MESH)

    l_sg.wait()
    signs_t = sg[...].astype(F32).astype(BF16)
    for i in range(4):
        enc_load(i).wait()

        def widen(j, c, i=i):
            e = pl.multiple_of(64 * i + 16 * j, 16)
            v = encb[pl.ds(e, 16)].astype(F32)
            for h in range(2):
                w = v[:, 8 * h : 8 * h + 8].reshape(128, 512)
                for b in range(4):
                    encf[h, b, pl.ds(pl.multiple_of(e * 8, 128), 128), :] = w[
                        :, 128 * b : 128 * b + 128
                    ]
            return c

        lax.fori_loop(0, 4, widen, 0)

    def decode(r, c):
        v = jnp.concatenate(
            [encf[r // 8, b, pl.ds(r % 8, 256, stride=8), :] for b in range(4)], axis=1
        ).astype(BF16)
        d = lax.dot_general(
            signs_t, v, (((1,), (0,)), ((), ())), preferred_element_type=F32
        )
        for b in range(4):
            part[pl.ds(b * 16 + r, 64, stride=64), :] = d[:, b * 128 : (b + 1) * 128]
        return c

    lax.fori_loop(0, 16, decode, 0, unroll=4)

    pl.semaphore_wait(barrier, 14)
    for d in range(1, 4):
        to = dev(x, (y + d) % 4, z, co)
        pl.semaphore_signal(ready, inc=1, device_id=to, device_id_type=MESH)

    def prow(t, h):
        return pl.ds(pl.multiple_of(1024 * t + CH * h, CH), CH)

    def sw_copy(i):
        zz = (1 - zl) if i < NCH else zl
        return rcopy(
            part.at[prow(2 * zz + 1 - co, i % NCH), :], rb.at[i],
            sw_s.at[i], sw_r.at[i], partner,
        )

    for i in range(2 * NCH):
        sw_copy(i).start()

    l_rx.wait()
    l_ap.wait()

    def conv(i, c):
        rows = pl.ds(pl.multiple_of(64 * i, 64), 64)
        rxs[0, rows, :] = rxi[0, rows, :].astype(F32).astype(BF16)
        rxs[1, rows, :] = rxi[1, rows, :].astype(F32).astype(BF16)
        return c

    lax.fori_loop(0, 16, conv, 0)
    own = pl.ds(pl.multiple_of(64 * g, 64), 64)
    rxa[g, 0] = rxs[0, own, :]
    rxa[g, 1] = rxs[1, own, :]
    half = pl.ds(pl.multiple_of(32 * co, 32), 32)
    step = 2 * zl - 1

    def rx_copy(i, to_y, to_z):
        gt = to_y * 4 + to_z // 2
        return rcopy(
            rxs.at[:, pl.ds(pl.multiple_of(64 * gt + 32 * co, 32), 32), :],
            rxa.at[g, :, half, :],
            rx_s.at[i], rx_r.at[g], dev(x, to_y, to_z, co),
        )

    def rx_start(i, c):
        d = jnp.where(i < 8, 1 + i % 2, 3)
        yy = jnp.where(i < 8, i // 2, i - 8)
        rx_copy(i, (y + yy + 1) % 4, (z + step * d + 8) % 8).start()
        return c

    def rx_start_y(i, c):
        rx_copy(12 + i, (y + 1 + i) % 4, z).start()
        return c


    def ze_copy(h):
        return rcopy(zs.at[h], zb.at[h], ze_s.at[h], ze_r.at[h], mate)

    def zc_copy(h):
        return rcopy(zsc.at[h], zbc.at[h], zc_s.at[h], zc_r.at[h], mate)

    for h in range(NCH):
        sw_copy(h).wait_recv()
        v = (part[prow(2 * (1 - zl) + co, h), :] + rb[h]).reshape(CH // 8, 8, 128)
        top = jnp.maximum(jnp.max(jnp.abs(v), axis=0), 1e-30)
        q = jnp.round(v * (32767.0 / top)[None]).astype(jnp.int32)
        zs[h] = q.reshape(CH, 128).astype(jnp.int16)
        zsc[h] = top * (1.0 / 32767.0)
        ze_copy(h).start()
        zc_copy(h).start()
        if h == 0:
            pl.semaphore_wait(ready, 3)
            lax.fori_loop(0, 8, rx_start, 0)
            lax.fori_loop(0, 3, rx_start_y, 0)
            lax.fori_loop(8, 12, rx_start, 0)

    def xg_copy(i, slot, h, to):
        ref = da.at[slot, pl.ds(CH * h, CH), :]
        return rcopy(ref, ref, xg_s.at[i], xg_r.at[i], to)

    def relay(h):
        if h == NCH - 1:
            return
        if h == 0:
            xg_copy(h, xl, h, right).wait_recv()
            xg_copy(2 * NCH + h, xl, h, right).start()
        else:
            xg_copy(NCH + h, xr, h, left).wait_recv()
            xg_copy(2 * NCH + h, xr, h, left).start()

    for h in range(NCH):
        sw_copy(NCH + h).wait_recv()
        ze_copy(h).wait_recv()
        zc_copy(h).wait_recv()
        v = zb[h].astype(jnp.int32).astype(F32).reshape(CH // 8, 8, 128) * zbc[h][None]
        tot = part[prow(tx, h), :] + rb[NCH + h] + v.reshape(CH, 128)
        da[x, pl.ds(CH * h, CH), :] = (tot * (1.0 / 1024)).astype(BF16)
        if h == NCH - 1:
            xg_copy(2 * NCH + h, x, h, across).start()
        xg_copy(h, x, h, right).start()
        xg_copy(NCH + h, x, h, left).start()
        if h > 0:
            relay(h - 1)
    relay(NCH - 1)

    def dz_of(i):
        return (ORDER_Z >> (2 * i)) & 3

    def dy_of(i):
        return (ORDER_Y >> (2 * i)) & 3

    def gt_of(i):
        return ((y + dy_of(i)) % 4) * 4 + (zh + dz_of(i)) % 4

    def fw_copy(gs):
        ref = rxa.at[gs, :, half, :]
        return rcopy(ref, ref, fw_s.at[gs], fw_r.at[gs], partner)

    def fw(i):
        gs = gt_of(i)
        pltpu.make_async_copy(
            rxa.at[gs, :, half, :], rxa.at[gs, :, half, :], rx_r.at[gs]
        ).wait()
        fw_copy(gs).start()

    def fw_first(i, c):
        fw(i)
        return c

    lax.fori_loop(0, AHEAD, fw_first, 0)

    def flip(k, acc):
        rows = pl.ds(pl.multiple_of(64 * k, 64), 64)
        v = jnp.concatenate([da[i, rows, :] for i in range(4)], axis=0).astype(F32)
        dt[pl.ds(pl.multiple_of(128 * k, 128), 128), :] = v.T.astype(BF16)
        return acc + v

    total = jnp.zeros((256, 128), F32)
    for h in range(NCH):
        if h == 0 or h == NCH - 1:
            xg_copy(NCH + h, xr, h, left).wait_recv()
        if h > 0:
            xg_copy(h, xl, h, right).wait_recv()
        xg_copy(2 * NCH + h, x, h, right).wait_recv()
        total = lax.fori_loop(h * (16 // NCH), (h + 1) * (16 // NCH), flip, total)
    pieces = []
    for i in range(4):
        d0, d1, d2 = (total[64 * i + 16 * b : 64 * i + 16 * b + 16] for b in range(3))
        pieces += [-(d0 + d1), -d1, jnp.zeros_like(d2), d2]
    base_t = jnp.concatenate(pieces, axis=0).T
    hi = base_t.astype(BF16)
    dt[2048:2176, :] = hi
    dt[2176:2304, :] = (base_t - hi.astype(F32)).astype(BF16)

    def fw_wait(i):
        gs = gt_of(i)
        oth = rxa.at[gs, :, pl.ds(pl.multiple_of(32 * (1 - co), 32), 32), :]
        pltpu.make_async_copy(oth, oth, fw_r.at[gs]).wait()

    for i in range(16):
        tx_load(i).wait()

    def ci_copy(i):
        return rcopy(send.at[i], ib.at[i], ci_s.at[i], ci_r.at[i], partner)

    def slot_of(i):
        d = dy_of(i)
        return dz_of(i) * 3 + jnp.where(d == 2, 0, jnp.where(d == 1, 1, 2))

    def y_copy(m, d):
        to = dev(x, (y + d) % 4, z, co)
        return rcopy(ys.at[m], yb.at[m], y_s.at[m], y_r.at[m], to)

    def z_copy(zt):
        d = (zt - z + 8) % 8 - 1
        return rcopy(zss.at[zt], zrb.at[d], z_s.at[d], z_r.at[d], dev(x, y, zt, co))

    def finish(i):
        ci_copy(i).wait_recv()

        @pl.when(dy_of(i) != 0)
        def _():
            m = slot_of(i)
            ys[m] = (keep[i] + ib[i]).astype(BF16)
            y_copy(m, dy_of(i)).start()

        @pl.when(dy_of(i) == 0)
        def _():
            n = dz_of(i)
            for d in range(3):
                y_copy(3 * n + d, 1).wait_recv()
            for q in range(2):
                tot = keep[i, q] + ib[i, q]
                for d in range(3):
                    tot = tot + yb[3 * n + d, q].astype(F32)
                zt = 2 * ((zh + n) % 4) + q
                zss[zt] = tot.astype(BF16)

                @pl.when(zt != z)
                def _(zt=zt):
                    z_copy(zt).start()

                @pl.when(zt == z)
                def _(tot=tot):
                    zown[...] = tot

    def block(i, c):
        gt = gt_of(i)

        @pl.when(i + AHEAD < 15)
        def _():
            fw(i + AHEAD)

        @pl.when(i < 15)
        def _():
            fw_wait(i)

        rxv = rxa[gt, 0].astype(F32)
        apv = rxa[gt, 1].astype(F32)
        v0 = jnp.where(rxv == 0.0, apv, 0.0)
        v1 = jnp.where(rxv == 1.0, apv, 0.0)
        v2 = jnp.where(rxv == 2.0, apv, 0.0)
        ws = (-v0, v0 - v1, v1 - v2, v2)
        w = jnp.concatenate(
            [ws[b][16 * i4 : 16 * i4 + 16] for i4 in range(4) for b in range(4)], axis=0
        ).astype(BF16)
        delta[...] = jnp.dot(dt[...], w, preferred_element_type=F32)
        t = txi[gt].astype(F32)
        for q in range(4):
            acc = (
                delta[2048 + 32 * q : 2080 + 32 * q, :] + delta[2176 + 32 * q : 2208 + 32 * q, :]
            )
            for k in range(16):
                acc = acc + t[k : k + 1] * delta[128 * k + 32 * q : 128 * k + 32 * q + 32, :]
            to_keep = (q % 2) == co

            @pl.when(to_keep)
            def _(acc=acc, q=q):
                keep[i, q // 2] = acc

            @pl.when(jnp.logical_not(to_keep))
            def _(acc=acc, q=q):
                send[i, q // 2] = acc

        ci_copy(i).start()

        @pl.when(i >= LAG)
        def _():
            finish(i - LAG)

        return c

    lax.fori_loop(0, 16, block, 0)
    for i in range(16 - LAG, 16):
        finish(i)

    for i in range(2 * NCH):
        sw_copy(i).wait_send()
    for h in range(NCH):
        ze_copy(h).wait_send()
        zc_copy(h).wait_send()

    def drain_rx(i, c):
        rx_copy(i, y, z).wait_send()
        fw_copy(gt_of(i)).wait_send()
        return c

    lax.fori_loop(0, 15, drain_rx, 0)
    for i in range(3 * NCH):
        xg_copy(i, x, i % NCH, right).wait_send()

    def drain_ci(i, c):
        ci_copy(i).wait_send()
        return c

    lax.fori_loop(0, 16, drain_ci, 0)

    def drain_y(i, c):
        y_copy(i, 1).wait_send()
        return c

    lax.fori_loop(0, 12, drain_y, 0)
    for d in range(1, 8):
        z_copy((z + d) % 8).wait_send()

    for d in range(1, 8):
        z_copy((z + d) % 8).wait_recv()
    tot = zown[...]
    for d in range(7):
        tot = tot + zrb[d].astype(F32)
    out_ref[...] = tot * 0.125


def on_device(encoded, signs, tx_block, rx_block, apodization):
    dma = pltpu.SemaphoreType.DMA
    hbm = pl.BlockSpec(memory_space=pl.ANY)
    return pl.pallas_call(
        kernel,
        out_shape=jax.ShapeDtypeStruct((32, 256), F32),
        in_specs=[hbm] * 5,
        out_specs=pl.BlockSpec(memory_space=pltpu.VMEM),
        scratch_shapes=[
            pltpu.VMEM((256, 16, 512), BF16),
            pltpu.VMEM((2, 4, 2048, 128), F32),
            pltpu.VMEM((64, 256), jnp.int32),
            pltpu.VMEM((4096, 128), F32),
            pltpu.VMEM((2 * NCH, CH, 128), F32),
            pltpu.VMEM((NCH, CH, 128), jnp.int16),
            pltpu.VMEM((NCH, CH, 128), jnp.int16),
            pltpu.VMEM((NCH, 8, 128), F32),
            pltpu.VMEM((NCH, 8, 128), F32),
            pltpu.VMEM((4, 1024, 128), BF16),
            pltpu.VMEM((2304, 256), BF16),
            pltpu.VMEM((2, 1024, 256), jnp.int32),
            pltpu.VMEM((2, 1024, 256), BF16),
            pltpu.VMEM((16, 2, 64, 256), BF16),
            pltpu.VMEM((16, 16, 256), jnp.int32),
            pltpu.VMEM((2304, 256), F32),
            pltpu.VMEM((16, 2, 32, 256), F32),
            pltpu.VMEM((16, 2, 32, 256), F32),
            pltpu.VMEM((16, 2, 32, 256), F32),
            pltpu.VMEM((12, 2, 32, 256), BF16),
            pltpu.VMEM((12, 2, 32, 256), BF16),
            pltpu.VMEM((8, 32, 256), BF16),
            pltpu.VMEM((7, 32, 256), BF16),
            pltpu.VMEM((32, 256), F32),
            dma((4,)), dma((2,)), dma, dma((16,)),
            dma((15,)), dma((16,)), dma((16,)), dma((16,)),
            dma((2 * NCH,)), dma((2 * NCH,)), dma((NCH,)), dma((NCH,)), dma((NCH,)), dma((NCH,)),
            dma((3 * NCH,)), dma((3 * NCH,)),
            dma((16,)), dma((16,)), dma((12,)), dma((12,)), dma((7,)), dma((7,)), pltpu.SemaphoreType.REGULAR,
        ],
        compiler_params=pltpu.CompilerParams(
            collective_id=0, has_side_effects=True, vmem_limit_bytes=60 * 1024 * 1024
        ),
    )(encoded, signs.T, tx_block, rx_block, apodization).T


def solution(mesh):
    placed = (P("tx", "img", None), P(), P("tx", None), P(None, "img"), P(None, "img"))
    return jax.shard_map(
        on_device, mesh=mesh, in_specs=placed, out_specs=P("img", "tx"), check_vma=False
    )
```

```python
import jax
import jax.numpy as jnp
from jax import lax
from jax.experimental import pallas as pl
from jax.experimental.pallas import tpu as pltpu
from jax.sharding import PartitionSpec as P

MESH = pl.DeviceIdType.MESH
F32 = jnp.float32
BF16 = jnp.bfloat16
LG = 256
NCH = 4
CH = 1024 // NCH
LAG = 3
AHEAD = 4


def packed(table):
    word = sum(v << (2 * i) for i, v in enumerate(table))
    return word - (1 << 32) if word >> 31 else word


ORDER_Z = packed((1,1,1,2,2,2,3,3,3,1,0,0,0,2,3,0))
ORDER_Y = packed((2,1,3,2,1,3,2,1,3,0,2,1,3,0,0,0))


def kernel(
    enc_hbm, signs_hbm, tx_hbm, rx_hbm, apo_hbm, out_ref,
    encb, encf, sg, part, rb, zs, zb, zsc, zbc, da, dt, rxi, rxs, rxa, txi,
    delta, keep, send, ib, ys, yb, zss, zrb, zown,
    ld_enc, ld_rx, ld_sg, ld_tx,
    rx_s, rx_r, fw_s, fw_r, sw_s, sw_r, ze_s, ze_r, zc_s, zc_r, xg_s, xg_r,
    ci_s, ci_r, y_s, y_r, z_s, z_r, ready,
):
    tx = lax.axis_index("tx")
    img = lax.axis_index("img")
    zl = tx // 2
    co = tx % 2
    y = img // 16
    zh = (img // 4) % 4
    x = img % 4
    z = zh * 2 + zl
    g = y * 4 + zh

    def dev(xx, yy, zz, cc):
        return {"tx": (zz % 2) * 2 + cc, "img": (yy * 4 + zz // 2) * 4 + xx}

    partner = dev(x, y, z, 1 - co)
    mate = dev(x, y, zh * 2 + (1 - zl), co)
    xr = (x + 1) % 4
    xl = (x + 3) % 4
    right = dev(xr, y, z, co)
    left = dev(xl, y, z, co)
    across = dev((x + 2) % 4, y, z, co)

    def rcopy(src, dst, ss, rs, to):
        return pltpu.make_async_remote_copy(
            src_ref=src, dst_ref=dst, send_sem=ss, recv_sem=rs,
            device_id=to, device_id_type=MESH,
        )

    def enc_load(i):
        return pltpu.make_async_copy(
            enc_hbm.at[pl.ds(64 * i, 64)], encb.at[pl.ds(64 * i, 64)], ld_enc.at[i]
        )

    l_rx = pltpu.make_async_copy(rx_hbm, rxi.at[0], ld_rx.at[0])
    l_ap = pltpu.make_async_copy(apo_hbm, rxi.at[1], ld_rx.at[1])
    l_sg = pltpu.make_async_copy(
        signs_hbm.at[:, pl.ds(pl.multiple_of(256 * tx, 256), 256)], sg, ld_sg
    )
    l_sg.start()
    for i in range(4):
        enc_load(i).start()
    l_rx.start()
    l_ap.start()

    def tx_load(i):
        return pltpu.make_async_copy(
            tx_hbm.at[:, pl.ds(pl.multiple_of(LG * (4 * i + x), LG), LG)],
            txi.at[i], ld_tx.at[i],
        )

    for i in range(16):
        tx_load(i).start()

    barrier = pltpu.get_barrier_semaphore()
    for to in (partner, right, left, across):
        pl.semaphore_signal(barrier, inc=1, device_id=to, device_id_type=MESH)

    for d in range(1, 4):
        to = dev(x, (y + d) % 4, z, co)
        pl.semaphore_signal(barrier, inc=1, device_id=to, device_id_type=MESH)
    for d in range(1, 8):
        to = dev(x, y, (z + d) % 8, co)
        pl.semaphore_signal(barrier, inc=1, device_id=to, device_id_type=MESH)

    l_sg.wait()
    signs_t = sg[...].astype(F32).astype(BF16)
    for i in range(4):
        enc_load(i).wait()

        def widen(j, c, i=i):
            e = pl.multiple_of(64 * i + 16 * j, 16)
            v = encb[pl.ds(e, 16)].astype(F32)
            for h in range(2):
                w = v[:, 8 * h : 8 * h + 8].reshape(128, 512)
                for b in range(4):
                    encf[h, b, pl.ds(pl.multiple_of(e * 8, 128), 128), :] = w[
                        :, 128 * b : 128 * b + 128
                    ]
            return c

        lax.fori_loop(0, 4, widen, 0)

    def decode(r, c):
        v = jnp.concatenate(
            [encf[r // 8, b, pl.ds(r % 8, 256, stride=8), :] for b in range(4)], axis=1
        ).astype(BF16)
        d = lax.dot_general(
            signs_t, v, (((1,), (0,)), ((), ())), preferred_element_type=F32
        )
        for b in range(4):
            part[pl.ds(b * 16 + r, 64, stride=64), :] = d[:, b * 128 : (b + 1) * 128]
        return c

    lax.fori_loop(0, 16, decode, 0, unroll=8)

    pl.semaphore_wait(barrier, 14)
    for d in range(1, 4):
        to = dev(x, (y + d) % 4, z, co)
        pl.semaphore_signal(ready, inc=1, device_id=to, device_id_type=MESH)

    def prow(t, h):
        return pl.ds(pl.multiple_of(1024 * t + CH * h, CH), CH)

    def sw_copy(i):
        zz = (1 - zl) if i < NCH else zl
        return rcopy(
            part.at[prow(2 * zz + 1 - co, i % NCH), :], rb.at[i],
            sw_s.at[i], sw_r.at[i], partner,
        )

    for i in range(2 * NCH):
        sw_copy(i).start()

    l_rx.wait()
    l_ap.wait()

    def conv(i, c):
        rows = pl.ds(pl.multiple_of(64 * i, 64), 64)
        rxs[0, rows, :] = rxi[0, rows, :].astype(F32).astype(BF16)
        rxs[1, rows, :] = rxi[1, rows, :].astype(F32).astype(BF16)
        return c

    lax.fori_loop(0, 16, conv, 0)
    own = pl.ds(pl.multiple_of(64 * g, 64), 64)
    rxa[g, 0] = rxs[0, own, :]
    rxa[g, 1] = rxs[1, own, :]
    half = pl.ds(pl.multiple_of(32 * co, 32), 32)
    step = 2 * zl - 1

    def rx_copy(i, to_y, to_z):
        gt = to_y * 4 + to_z // 2
        return rcopy(
            rxs.at[:, pl.ds(pl.multiple_of(64 * gt + 32 * co, 32), 32), :],
            rxa.at[g, :, half, :],
            rx_s.at[i], rx_r.at[g], dev(x, to_y, to_z, co),
        )

    def rx_start(i, c):
        d = jnp.where(i < 8, 1 + i % 2, 3)
        yy = jnp.where(i < 8, i // 2, i - 8)
        rx_copy(i, (y + yy + 1) % 4, (z + step * d + 8) % 8).start()
        return c

    def rx_start_y(i, c):
        rx_copy(12 + i, (y + 1 + i) % 4, z).start()
        return c


    def ze_copy(h):
        return rcopy(zs.at[h], zb.at[h], ze_s.at[h], ze_r.at[h], mate)

    def zc_copy(h):
        return rcopy(zsc.at[h], zbc.at[h], zc_s.at[h], zc_r.at[h], mate)

    for h in range(NCH):
        sw_copy(h).wait_recv()
        v = (part[prow(2 * (1 - zl) + co, h), :] + rb[h]).reshape(CH // 8, 8, 128)
        top = jnp.maximum(jnp.max(jnp.abs(v), axis=0), 1e-30)
        q = jnp.round(v * (32767.0 / top)[None]).astype(jnp.int32)
        zs[h] = q.reshape(CH, 128).astype(jnp.int16)
        zsc[h] = top * (1.0 / 32767.0)
        ze_copy(h).start()
        zc_copy(h).start()
        if h == 0:
            pl.semaphore_wait(ready, 3)
            lax.fori_loop(0, 8, rx_start, 0)
            lax.fori_loop(0, 3, rx_start_y, 0)
            lax.fori_loop(8, 12, rx_start, 0)

    def xg_copy(i, slot, h, to):
        ref = da.at[slot, pl.ds(CH * h, CH), :]
        return rcopy(ref, ref, xg_s.at[i], xg_r.at[i], to)

    def relay(h):
        if h == NCH - 1:
            return
        if h == 0:
            xg_copy(h, xl, h, right).wait_recv()
            xg_copy(2 * NCH + h, xl, h, right).start()
        else:
            xg_copy(NCH + h, xr, h, left).wait_recv()
            xg_copy(2 * NCH + h, xr, h, left).start()

    for h in range(NCH):
        sw_copy(NCH + h).wait_recv()
        ze_copy(h).wait_recv()
        zc_copy(h).wait_recv()
        v = zb[h].astype(jnp.int32).astype(F32).reshape(CH // 8, 8, 128) * zbc[h][None]
        tot = part[prow(tx, h), :] + rb[NCH + h] + v.reshape(CH, 128)
        da[x, pl.ds(CH * h, CH), :] = (tot * (1.0 / 1024)).astype(BF16)
        if h == NCH - 1:
            xg_copy(2 * NCH + h, x, h, across).start()
        xg_copy(h, x, h, right).start()
        xg_copy(NCH + h, x, h, left).start()
        if h > 0:
            relay(h - 1)
    relay(NCH - 1)

    def dz_of(i):
        return (ORDER_Z >> (2 * i)) & 3

    def dy_of(i):
        return (ORDER_Y >> (2 * i)) & 3

    def gt_of(i):
        return ((y + dy_of(i)) % 4) * 4 + (zh + dz_of(i)) % 4

    def fw_copy(gs):
        ref = rxa.at[gs, :, half, :]
        return rcopy(ref, ref, fw_s.at[gs], fw_r.at[gs], partner)

    def fw(i):
        gs = gt_of(i)
        pltpu.make_async_copy(
            rxa.at[gs, :, half, :], rxa.at[gs, :, half, :], rx_r.at[gs]
        ).wait()
        fw_copy(gs).start()

    def fw_first(i, c):
        fw(i)
        return c

    lax.fori_loop(0, AHEAD, fw_first, 0)

    def flip(k, acc):
        rows = pl.ds(pl.multiple_of(64 * k, 64), 64)
        v = jnp.concatenate([da[i, rows, :] for i in range(4)], axis=0).astype(F32)
        dt[pl.ds(pl.multiple_of(128 * k, 128), 128), :] = v.T.astype(BF16)
        return acc + v

    total = jnp.zeros((256, 128), F32)
    for h in range(NCH):
        if h == 0 or h == NCH - 1:
            xg_copy(NCH + h, xr, h, left).wait_recv()
        if h > 0:
            xg_copy(h, xl, h, right).wait_recv()
        xg_copy(2 * NCH + h, x, h, right).wait_recv()
        total = lax.fori_loop(h * (16 // NCH), (h + 1) * (16 // NCH), flip, total)
    pieces = []
    for i in range(4):
        d0, d1, d2 = (total[64 * i + 16 * b : 64 * i + 16 * b + 16] for b in range(3))
        pieces += [-(d0 + d1), -d1, jnp.zeros_like(d2), d2]
    base_t = jnp.concatenate(pieces, axis=0).T
    hi = base_t.astype(BF16)
    dt[2048:2176, :] = hi
    dt[2176:2304, :] = (base_t - hi.astype(F32)).astype(BF16)

    def fw_wait(i):
        gs = gt_of(i)
        oth = rxa.at[gs, :, pl.ds(pl.multiple_of(32 * (1 - co), 32), 32), :]
        pltpu.make_async_copy(oth, oth, fw_r.at[gs]).wait()

    for i in range(16):
        tx_load(i).wait()

    def ci_copy(i):
        return rcopy(send.at[i], ib.at[i], ci_s.at[i], ci_r.at[i], partner)

    def slot_of(i):
        d = dy_of(i)
        return dz_of(i) * 3 + jnp.where(d == 2, 0, jnp.where(d == 1, 1, 2))

    def y_copy(m, d):
        to = dev(x, (y + d) % 4, z, co)
        return rcopy(ys.at[m], yb.at[m], y_s.at[m], y_r.at[m], to)

    def z_copy(zt):
        d = (zt - z + 8) % 8 - 1
        return rcopy(zss.at[zt], zrb.at[d], z_s.at[d], z_r.at[d], dev(x, y, zt, co))

    def finish(i):
        ci_copy(i).wait_recv()

        @pl.when(dy_of(i) != 0)
        def _():
            m = slot_of(i)
            ys[m] = (keep[i] + ib[i]).astype(BF16)
            y_copy(m, dy_of(i)).start()

        @pl.when(dy_of(i) == 0)
        def _():
            n = dz_of(i)
            for d in range(3):
                y_copy(3 * n + d, 1).wait_recv()
            for q in range(2):
                tot = keep[i, q] + ib[i, q]
                for d in range(3):
                    tot = tot + yb[3 * n + d, q].astype(F32)
                zt = 2 * ((zh + n) % 4) + q
                zss[zt] = tot.astype(BF16)

                @pl.when(zt != z)
                def _(zt=zt):
                    z_copy(zt).start()

                @pl.when(zt == z)
                def _(tot=tot):
                    zown[...] = tot

    def block(i, c):
        gt = gt_of(i)

        @pl.when(i + AHEAD < 15)
        def _():
            fw(i + AHEAD)

        @pl.when(i < 15)
        def _():
            fw_wait(i)

        rxv = rxa[gt, 0].astype(F32)
        apv = rxa[gt, 1].astype(F32)
        v0 = jnp.where(rxv == 0.0, apv, 0.0)
        v1 = jnp.where(rxv == 1.0, apv, 0.0)
        v2 = jnp.where(rxv == 2.0, apv, 0.0)
        ws = (-v0, v0 - v1, v1 - v2, v2)
        w = jnp.concatenate(
            [ws[b][16 * i4 : 16 * i4 + 16] for i4 in range(4) for b in range(4)], axis=0
        ).astype(BF16)
        delta[...] = jnp.dot(dt[...], w, preferred_element_type=F32)
        t = txi[gt].astype(F32)
        for q in range(4):
            acc = (
                delta[2048 + 32 * q : 2080 + 32 * q, :] + delta[2176 + 32 * q : 2208 + 32 * q, :]
            )
            for k in range(16):
                acc = acc + t[k : k + 1] * delta[128 * k + 32 * q : 128 * k + 32 * q + 32, :]
            to_keep = (q % 2) == co

            @pl.when(to_keep)
            def _(acc=acc, q=q):
                keep[i, q // 2] = acc

            @pl.when(jnp.logical_not(to_keep))
            def _(acc=acc, q=q):
                send[i, q // 2] = acc

        ci_copy(i).start()

        @pl.when(i >= LAG)
        def _():
            finish(i - LAG)

        return c

    lax.fori_loop(0, 16, block, 0)
    for i in range(16 - LAG, 16):
        finish(i)

    for i in range(2 * NCH):
        sw_copy(i).wait_send()
    for h in range(NCH):
        ze_copy(h).wait_send()
        zc_copy(h).wait_send()

    def drain_rx(i, c):
        rx_copy(i, y, z).wait_send()
        fw_copy(gt_of(i)).wait_send()
        return c

    lax.fori_loop(0, 15, drain_rx, 0)
    for i in range(3 * NCH):
        xg_copy(i, x, i % NCH, right).wait_send()

    def drain_ci(i, c):
        ci_copy(i).wait_send()
        return c

    lax.fori_loop(0, 16, drain_ci, 0)

    def drain_y(i, c):
        y_copy(i, 1).wait_send()
        return c

    lax.fori_loop(0, 12, drain_y, 0)
    for d in range(1, 8):
        z_copy((z + d) % 8).wait_send()

    for d in range(1, 8):
        z_copy((z + d) % 8).wait_recv()
    tot = zown[...]
    for d in range(7):
        tot = tot + zrb[d].astype(F32)
    out_ref[...] = tot * 0.125


def on_device(encoded, signs, tx_block, rx_block, apodization):
    dma = pltpu.SemaphoreType.DMA
    hbm = pl.BlockSpec(memory_space=pl.ANY)
    return pl.pallas_call(
        kernel,
        out_shape=jax.ShapeDtypeStruct((32, 256), F32),
        in_specs=[hbm] * 5,
        out_specs=pl.BlockSpec(memory_space=pltpu.VMEM),
        scratch_shapes=[
            pltpu.VMEM((256, 16, 512), BF16),
            pltpu.VMEM((2, 4, 2048, 128), F32),
            pltpu.VMEM((64, 256), jnp.int32),
            pltpu.VMEM((4096, 128), F32),
            pltpu.VMEM((2 * NCH, CH, 128), F32),
            pltpu.VMEM((NCH, CH, 128), jnp.int16),
            pltpu.VMEM((NCH, CH, 128), jnp.int16),
            pltpu.VMEM((NCH, 8, 128), F32),
            pltpu.VMEM((NCH, 8, 128), F32),
            pltpu.VMEM((4, 1024, 128), BF16),
            pltpu.VMEM((2304, 256), BF16),
            pltpu.VMEM((2, 1024, 256), jnp.int32),
            pltpu.VMEM((2, 1024, 256), BF16),
            pltpu.VMEM((16, 2, 64, 256), BF16),
            pltpu.VMEM((16, 16, 256), jnp.int32),
            pltpu.VMEM((2304, 256), F32),
            pltpu.VMEM((16, 2, 32, 256), F32),
            pltpu.VMEM((16, 2, 32, 256), F32),
            pltpu.VMEM((16, 2, 32, 256), F32),
            pltpu.VMEM((12, 2, 32, 256), BF16),
            pltpu.VMEM((12, 2, 32, 256), BF16),
            pltpu.VMEM((8, 32, 256), BF16),
            pltpu.VMEM((7, 32, 256), BF16),
            pltpu.VMEM((32, 256), F32),
            dma((4,)), dma((2,)), dma, dma((16,)),
            dma((15,)), dma((16,)), dma((16,)), dma((16,)),
            dma((2 * NCH,)), dma((2 * NCH,)), dma((NCH,)), dma((NCH,)), dma((NCH,)), dma((NCH,)),
            dma((3 * NCH,)), dma((3 * NCH,)),
            dma((16,)), dma((16,)), dma((12,)), dma((12,)), dma((7,)), dma((7,)), pltpu.SemaphoreType.REGULAR,
        ],
        compiler_params=pltpu.CompilerParams(
            collective_id=0, has_side_effects=True, vmem_limit_bytes=60 * 1024 * 1024
        ),
    )(encoded, signs.T, tx_block, rx_block, apodization).T


def solution(mesh):
    placed = (P("tx", "img", None), P(), P("tx", None), P(None, "img"), P(None, "img"))
    return jax.shard_map(
        on_device, mesh=mesh, in_specs=placed, out_specs=P("img", "tx"), check_vma=False
    )
```
